256 devices in a mesh: orient: 2 (over x_hi), slab: 128 (over y, x_lo, z, core).
Axes of the slice: x: 4 (x_hi: 2, x_lo: 2; x = x_hi * 2 + x_lo), y: 4, z: 8, core: 2. Of those that a mesh axis runs over, the one named last changes fastest.
Arguments:
- propagator: float32 [64, 128, 128, 128], P('orient', 'slab'), may hold values from 0.2 to 2
- field: float32 [128, 128, 128], P('slab'), may hold values from -12 to 12
- orientations: float32 [3, 64], replicated, may hold values from -1 to 1, as said below
- weights: float32 [64], replicated, may hold values from 0.05 to 0.16
Outputs:
- propagated: float32 [64, 128, 128, 128], P('orient', 'slab')
The draws below stay inside these ranges and needn't reach their ends.
Inputs may be any that keep to these rules, and one draw needn't show every extreme that they name: Each column of orientations is a unit vector.
All inputs are finite; a program needn't handle non-finite values.
Results may differ from the reference program's by a relative error of at most 0.00024.
Values sent between devices are 32-bit elements; how exact they have to be, the bound alone decides.
No kernel may reach another device: no remote copies, remote signals or barrier semaphores. Data moves between devices by JAX's collectives and lax.ppermute only.
A program may use at most 64 MiB of HBM per device.

```python
import math
import jax
import jax.numpy as jnp
from jax import lax

NO = 64
LMAX = 10
NX = 128
NY = 128
NZ = 128


def draw_orientations(key, part):
    vectors = jax.random.normal(key, (3, NO), jnp.float32)
    return vectors / jnp.sqrt(jnp.sum(vectors * vectors, axis=0, keepdims=True))


def block_scale(own_key, dims, cuts, low, top_value):
    level, own = 1.0, jax.random.fold_in(own_key, 6)
    for dim, shards_of in cuts:
        draws = jnp.exp(jax.random.uniform(jax.random.fold_in(own, dim), (shards_of,), jnp.float32, low / len(cuts), top_value / len(cuts)))
        level = level * jnp.repeat(draws, dims[dim] // shards_of).reshape([-1 if axis == dim else 1 for axis in range(len(dims))])
    return level


def noise(key, dims, width, limit, split=(), held_as=jnp.bfloat16):
    array = width * jax.random.normal(key, dims, jnp.float32)
    if split:
        array = array * block_scale(key, dims, split, -0.22, 0.18)
    return jnp.clip(array, -limit, limit).astype(held_as)


def setup_inputs(seed: int = 0) -> dict:
    streams_of = jax.random.split(jax.random.key(seed), 5)
    return {
        "propagator": jnp.clip(0.2 + 1.8 * jax.random.uniform(streams_of[0], (NO, NZ, NY, NX), jnp.float32) ** block_scale(streams_of[0], (NO, NZ, NY, NX), ((0, 2), (1, 128)), -0.2, 0.2), 0.2, 2.0),
        "field": noise(streams_of[1], (NZ, NY, NX), 3.0, 12.0, ((0, 128),), jnp.float32),
        "orientations": draw_orientations(jax.random.fold_in(streams_of[4], 71), 0),
        "weights": jnp.clip(jax.random.uniform(streams_of[3], (NO,), jnp.float32, 0.05, 0.16), 0.05, 0.16),
    }


HALF_STEP = 0.1
BOX_LENGTH = 12.8
DECAY_RATE = 0.01


def wavenumbers(length):
    positions = jnp.arange(length, dtype=jnp.int32)
    signed = jnp.where(positions < length // 2, positions, positions - length)
    signed = jnp.where(positions == length // 2, 0, signed)
    return signed.astype(jnp.float32) * (2.0 * math.pi / BOX_LENGTH)


def mixing_matrix(orientations, weights):
    cosines = jnp.dot(orientations.T, orientations, precision=lax.Precision.HIGHEST)
    previous = jnp.ones_like(cosines)
    current = cosines
    combined = previous * (1.0 / (4.0 * math.pi))
    for degree in range(1, LMAX + 1):
        if degree > 1:
            previous, current = current, ((2 * degree - 1) * cosines * current - (degree - 1) * previous) / degree
        combined = combined + (math.exp(-DECAY_RATE * degree * (degree + 1)) * (2 * degree + 1) / (4.0 * math.pi)) * current
    return combined * weights[None, :]


def reference(propagator, field, orientations, weights):
    damping = jnp.exp(-0.5 * HALF_STEP * field)[None]
    damped = propagator * damping
    wave_z = wavenumbers(NZ)
    wave_y = wavenumbers(NY)
    wave_x = wavenumbers(NX)

    def advect_one(members):
        subblock, direction = members
        angles = HALF_STEP * (direction[0] * wave_x[None, None, :] + direction[1] * wave_y[None, :, None] + direction[2] * wave_z[:, None, None])
        spectrum = jnp.fft.fftn(subblock) * jnp.exp(-1j * angles)
        return jnp.real(jnp.fft.ifftn(spectrum))

    advected = lax.map(advect_one, (damped, orientations.T))
    prepared = advected * damping
    matrix = mixing_matrix(orientations, weights)
    flattened = prepared.reshape(prepared.shape[0], -1)
    return jnp.dot(matrix, flattened, precision=lax.Precision.HIGHEST).reshape(prepared.shape)
```

```python
import math

import jax
import jax.numpy as jnp
from jax import lax
from jax.sharding import PartitionSpec as P

LMAX = 10


HALF_STEP = 0.1
BOX_LENGTH = 12.8
DECAY_RATE = 0.01
HIGHEST = lax.Precision.HIGHEST
HIGH = lax.Precision.HIGH
AXES = ("orient", "slab")


def packed_tables(length):
    half = length // 2
    positions = jnp.arange(length, dtype=jnp.int32)
    orders = jnp.arange(half, dtype=jnp.int32)
    angles = (positions[:, None] * orders[None, :] % length).astype(jnp.float32) * (2.0 * math.pi / length)
    nyquist = jnp.where(positions % 2 == 0, 1.0, -1.0).astype(jnp.float32)
    sines = jnp.where(orders[None, :] == 0, nyquist[:, None], jnp.sin(angles))
    forward = jnp.concatenate([jnp.cos(angles), sines], axis=1)
    scale = jnp.where(jnp.arange(length) % half == 0, 1.0, 2.0).astype(jnp.float32) / length
    return forward, forward * scale[None, :]


def phase_tables(components, length):
    step = HALF_STEP * 2.0 * math.pi / BOX_LENGTH
    angles = components[:, None] * (jnp.arange(length // 2, dtype=jnp.float32) * step)[None, :]
    return jnp.cos(angles), jnp.sin(angles)


def shift_matrices(components, length):
    half = length // 2
    forward, inverse = packed_tables(length)
    cosines, sines = phase_tables(components, length)
    left_cos, left_sin = inverse[None, :, :half], inverse[None, :, half:]
    rotated = jnp.concatenate(
        [
            left_cos * cosines[:, None, :] + left_sin * sines[:, None, :],
            left_sin * cosines[:, None, :] - left_cos * sines[:, None, :],
        ],
        axis=2,
    )
    return jnp.einsum("oik,jk->oij", rotated, forward, precision=HIGH)


def mixing_matrix(orientations, weights):
    cosines = jnp.dot(orientations.T, orientations, precision=HIGHEST)
    previous = jnp.ones_like(cosines)
    current = cosines
    combined = previous * (1.0 / (4.0 * math.pi))
    for degree in range(1, LMAX + 1):
        if degree > 1:
            previous, current = (
                current,
                ((2 * degree - 1) * cosines * current - (degree - 1) * previous) / degree,
            )
        combined = (
            combined
            + math.exp(-DECAY_RATE * degree * (degree + 1))
            * (2 * degree + 1)
            / (4.0 * math.pi)
            * current
        )
    return combined * weights[None, :]


def local(propagator, field, orientations, weights):
    own, depth, rows, cols = propagator.shape
    groups = lax.axis_size("orient")
    slabs = lax.axis_size("slab")
    start = lax.axis_index("orient") * own
    directions = lax.dynamic_slice_in_dim(orientations, start, own, 1)
    damping = jnp.exp(-0.5 * HALF_STEP * field[0])
    damped = propagator[:, 0] * damping[None]
    shift_x = shift_matrices(directions[0], cols)
    shift_y = shift_matrices(directions[1], rows)
    moved = jnp.einsum("oyx,oix->oyi", damped, shift_x, precision=HIGH)
    moved = jnp.einsum("ojy,oyi->oji", shift_y, moved, precision=HIGH)
    width = cols // groups
    sent = moved.reshape(own, slabs, groups, width).transpose(2, 1, 0, 3).reshape(groups * slabs, own * width)
    lines = lax.all_to_all(sent, AXES, 0, 0, tiled=True)
    total_z = depth * slabs
    lines = lines.reshape(groups, total_z, own, width)
    forward, inverse = packed_tables(total_z)
    half = total_z // 2
    spectrum = jnp.einsum("hzow,zk->khow", lines, forward, precision=HIGH)
    cosines, sines = phase_tables(orientations[2], total_z)
    cosines = cosines.T.reshape(half, groups, own, 1)
    sines = sines.T.reshape(half, groups, own, 1)
    first, second = spectrum[:half], spectrum[half:]
    spectrum = jnp.concatenate(
        [first * cosines - second * sines, first * sines + second * cosines], axis=0
    )
    advected = jnp.einsum("khow,zk->hozw", spectrum, inverse, precision=HIGH)
    matrix = mixing_matrix(orientations, weights)
    mixed = jnp.dot(matrix, advected.reshape(groups * own, total_z * width), precision=HIGH)
    back = mixed.reshape(groups, own, total_z, width).transpose(0, 2, 1, 3).reshape(groups * slabs, own * width)
    final = lax.all_to_all(back, AXES, 0, 0, tiled=True)
    final = final.reshape(groups, slabs, own, width).transpose(2, 1, 0, 3).reshape(own, 1, rows, cols)
    return final * damping[None, None]


def solution(mesh):
    in_specs = (P("orient", "slab", None, None), P("slab", None, None), P(), P())
    out_specs = P("orient", "slab", None, None)
    return jax.shard_map(local, mesh=mesh, in_specs=in_specs, out_specs=out_specs, check_vma=False)
```

```python
import functools
import math

import jax
import jax.numpy as jnp
import numpy as np
from jax import lax
from jax.experimental import pallas as pl
from jax.experimental.pallas import tpu as pltpu
from jax.sharding import PartitionSpec as P

LMAX = 10


HALF_STEP = 0.1
BOX_LENGTH = 12.8
DECAY_RATE = 0.01
HIGHEST = lax.Precision.HIGHEST
AXES = ("orient", "slab")
INTERPRET = False


def packed_tables(length):
    half = length // 2
    positions = np.arange(length)
    orders = np.arange(half)
    angles = (positions[:, None] * orders[None, :] % length) * (2.0 * math.pi / length)
    nyquist = np.where(positions % 2 == 0, 1.0, -1.0)
    sines = np.where(orders[None, :] == 0, nyquist[:, None], np.sin(angles))
    forward = np.concatenate([np.cos(angles), sines], axis=1)
    scale = np.where(np.arange(length) % half == 0, 1.0, 2.0) / length
    return forward.astype(np.float32), (forward * scale[None, :]).astype(np.float32)


def phase_tables(components, length):
    step = HALF_STEP * 2.0 * math.pi / BOX_LENGTH
    angles = components[:, None] * (jnp.arange(length // 2, dtype=jnp.float32) * step)[None, :]
    return jnp.cos(angles), jnp.sin(angles)


def shift_kernels(components, length):
    half = length // 2
    _, inverse = packed_tables(length)
    cosines, sines = phase_tables(components, length)
    sines = jnp.where(jnp.arange(half)[None, :] == 0, 1.0, sines)
    return jnp.dot(jnp.concatenate([cosines, sines], axis=1), jnp.asarray(inverse.T), precision=HIGHEST)


def mixing_matrix(orientations, weights):
    cosines = jnp.dot(orientations.T, orientations, precision=HIGHEST)
    previous = jnp.ones_like(cosines)
    current = cosines
    combined = previous * (1.0 / (4.0 * math.pi))
    for degree in range(1, LMAX + 1):
        if degree > 1:
            previous, current = (
                current,
                ((2 * degree - 1) * cosines * current - (degree - 1) * previous) / degree,
            )
        combined = (
            combined
            + math.exp(-DECAY_RATE * degree * (degree + 1))
            * (2 * degree + 1)
            / (4.0 * math.pi)
            * current
        )
    return combined * weights[None, :]


def halves(values):
    high = values.astype(jnp.bfloat16)
    return high, (values - high.astype(jnp.float32)).astype(jnp.bfloat16)


def wide_table(values):
    high = values.astype(jnp.bfloat16)
    low = (values - high.astype(np.float32)).astype(jnp.bfloat16)
    return np.concatenate([high, high, low], axis=1)


def wide_left(values):
    high, low = halves(values)
    return jnp.concatenate([high, high, low], axis=1)


def wide_right(values):
    high, low = halves(values)
    return jnp.concatenate([high, low, high], axis=0)


def product(left, right):
    return jnp.dot(left, right, preferred_element_type=jnp.float32)


def swap(values):
    return pltpu.roll(values, values.shape[1] // 2, 1)


def low_lanes(shape):
    return lax.broadcasted_iota(jnp.int32, shape, 1) < shape[1] // 2


def circulant(row):
    length = row.shape[1]
    return pltpu.roll(jnp.broadcast_to(row, (length, length)), 0, 1, stride=1, stride_axis=0)


def plane_kernel(propagator_ref, field_ref, kernel_x_ref, kernel_y_ref, out_ref, damping_ref):
    row = pl.program_id(0)
    count = pl.num_programs(0)

    @pl.when(row == 0)
    def _():
        damping_ref[...] = jnp.exp(-0.5 * HALF_STEP * field_ref[...])

    moved = []
    for part in range(2):
        own = part * count + row
        damped = propagator_ref[part, 0] * damping_ref[...]
        shift_x = circulant(kernel_x_ref[pl.ds(own, 1), :])
        shift_y = circulant(kernel_y_ref[pl.ds(own, 1), :])
        along_x = product(wide_left(damped), wide_right(shift_x))
        moved.append(product(wide_left(shift_y), wide_right(along_x)))
    first, second = moved
    low = low_lanes(first.shape)
    rows = pl.ds(row, first.shape[0], stride=count)
    out_ref[0, rows, :] = jnp.where(low, first, swap(second))
    out_ref[1, rows, :] = jnp.where(low, swap(first), second)


def line_kernel(depth, lines_ref, forward_ref, inverse_ref, cos_ref, sin_ref, mixing_ref, out_ref, advected_ref):
    count = lines_ref.shape[1] // depth
    half = depth // 2
    lanes = lines_ref.shape[2]
    pairs = count // 2

    def shift(item, carry):
        group = item // pairs
        row = 2 * (item % pairs)
        taken = [lines_ref[group, pl.ds(row + n, depth, stride=count), :] for n in range(2)]
        spectrum = product(forward_ref[...], wide_right(jnp.concatenate(taken, axis=1)))
        cosines = jnp.concatenate([cos_ref[group, row + n] for n in range(2)], axis=1)
        sines = jnp.concatenate([sin_ref[group, row + n] for n in range(2)], axis=1)
        real, imaginary = spectrum[:half], spectrum[half:]
        turned = jnp.concatenate(
            [real * cosines - imaginary * sines, real * sines + imaginary * cosines], axis=0
        )
        advected = product(inverse_ref[...], wide_right(turned))
        for n in range(2):
            rows = pl.ds(group * count + row + n, depth, stride=2 * count)
            advected_ref[rows, :] = advected[:, n * lanes : (n + 1) * lanes]
        return carry

    lax.fori_loop(0, 2 * pairs, shift, 0)
    both = 2 * count
    mixing = wide_left(mixing_ref[...])
    low = low_lanes((both, lanes))

    def mix(step, carry):
        stacked = []
        for n in range(2):
            base = (4 * step + 2 * n) * both
            first = advected_ref[pl.ds(base, both), :]
            second = advected_ref[pl.ds(base + both, both), :]
            stacked.append(
                jnp.concatenate(
                    [jnp.where(low, first, swap(second)), jnp.where(low, swap(first), second)], axis=0
                )
            )
        mixed = product(mixing, wide_right(jnp.concatenate(stacked, axis=1)))
        for n in range(2):
            place = mixed[:, n * lanes : (n + 1) * lanes]
            first, second = place[:both], place[both:]
            for m, values in enumerate(
                (jnp.where(low, first, swap(second)), jnp.where(low, swap(first), second))
            ):
                target = pl.ds((4 * step + 2 * n + m) * count, count)
                out_ref[0, target, :] = values[:count]
                out_ref[1, target, :] = values[count:]
        return carry

    lax.fori_loop(0, depth // 4, mix, 0)


def close_kernel(mixed_ref, field_ref, out_ref, damping_ref):
    row = pl.program_id(0)
    count = pl.num_programs(0)

    @pl.when(row == 0)
    def _():
        damping_ref[...] = jnp.exp(-0.5 * HALF_STEP * field_ref[...])

    depth = field_ref.shape[0]
    first = mixed_ref[0, pl.ds(row, depth, stride=count), :]
    second = mixed_ref[1, pl.ds(row, depth, stride=count), :]
    low = low_lanes(first.shape)
    damping = damping_ref[...]
    out_ref[0, 0] = jnp.where(low, first, swap(second)) * damping
    out_ref[1, 0] = jnp.where(low, swap(first), second) * damping


def whole(shape):
    return pl.BlockSpec(shape, lambda row: (0,) * len(shape))


def local(propagator, field, orientations, weights):
    own, depth, rows, cols = propagator.shape
    groups = lax.axis_size("orient")
    slabs = lax.axis_size("slab")
    total_z = depth * slabs
    count = own // 2
    half = total_z // 2
    start = lax.axis_index("orient") * own
    directions = lax.dynamic_slice_in_dim(orientations, start, own, 1)
    kernel_x = shift_kernels(directions[0], cols)
    kernel_y = shift_kernels(-directions[1], rows)
    plane = field[0]
    message = (groups, slabs * count, cols)
    sent = pl.pallas_call(
        plane_kernel,
        grid=(count,),
        in_specs=[
            pl.BlockSpec((2, 1, rows, cols), lambda row: (0, row, 0, 0)),
            whole((rows, cols)),
            whole((own, cols)),
            whole((own, rows)),
        ],
        out_specs=whole(message),
        out_shape=jax.ShapeDtypeStruct(message, jnp.float32),
        scratch_shapes=[pltpu.VMEM((rows, cols), jnp.float32)],
        interpret=INTERPRET,
        name="plane",
    )(propagator.reshape(2, count, rows, cols), plane, kernel_x, kernel_y)

    lines = lax.all_to_all(sent.reshape(groups * slabs, count, cols), AXES, 0, 0, tiled=True)

    forward, inverse = packed_tables(total_z)
    cosines, sines = phase_tables(orientations[2], total_z)

    def by_lane(table):
        table = table.reshape(groups, 2, count, half).transpose(0, 2, 3, 1)
        return jnp.repeat(table, cols // 2, axis=3)

    matrix = mixing_matrix(orientations, weights)
    matrix = matrix.reshape(groups, 2, count, groups, 2, count).transpose(1, 0, 2, 4, 3, 5)
    matrix = matrix.reshape(2 * own, 2 * own)
    back = pl.pallas_call(
        functools.partial(line_kernel, total_z),
        out_shape=jax.ShapeDtypeStruct(message, jnp.float32),
        scratch_shapes=[pltpu.VMEM((total_z * groups * count, cols), jnp.float32)],
        interpret=INTERPRET,
        name="line",
    )(
        lines.reshape(message),
        wide_table(forward.T),
        wide_table(inverse),
        by_lane(cosines),
        by_lane(sines),
        matrix,
    )
    mixed = lax.all_to_all(back.reshape(groups * slabs, count, cols), AXES, 0, 0, tiled=True)
    result = pl.pallas_call(
        close_kernel,
        grid=(count,),
        in_specs=[whole(message), whole((rows, cols))],
        out_specs=pl.BlockSpec((2, 1, rows, cols), lambda row: (0, row, 0, 0)),
        out_shape=jax.ShapeDtypeStruct((2, count, rows, cols), jnp.float32),
        scratch_shapes=[pltpu.VMEM((rows, cols), jnp.float32)],
        interpret=INTERPRET,
        name="close",
    )(mixed.reshape(message), plane)
    return result.reshape(own, 1, rows, cols)


def solution(mesh):
    in_specs = (P("orient", "slab", None, None), P("slab", None, None), P(), P())
    out_specs = P("orient", "slab", None, None)
    return jax.shard_map(local, mesh=mesh, in_specs=in_specs, out_specs=out_specs, check_vma=False)
```

```python
import functools
import math

import jax
import jax.numpy as jnp
import numpy as np
from jax import lax
from jax.experimental import pallas as pl
from jax.experimental.pallas import tpu as pltpu
from jax.sharding import PartitionSpec as P

LMAX = 10


HALF_STEP = 0.1
BOX_LENGTH = 12.8
DECAY_RATE = 0.01
HIGHEST = lax.Precision.HIGHEST
AXES = ("orient", "slab")
PARAMS = pltpu.CompilerParams(vmem_limit_bytes=24 * 1024 * 1024)
UNROLL = 4


def packed_tables(length):
    half = length // 2
    positions = np.arange(length)
    orders = np.arange(half)
    angles = (positions[:, None] * orders[None, :] % length) * (2.0 * math.pi / length)
    nyquist = np.where(positions % 2 == 0, 1.0, -1.0)
    sines = np.where(orders[None, :] == 0, nyquist[:, None], np.sin(angles))
    forward = np.concatenate([np.cos(angles), sines], axis=1)
    scale = np.where(np.arange(length) % half == 0, 1.0, 2.0) / length
    return forward.astype(np.float32), (forward * scale[None, :]).astype(np.float32)


def phase_tables(components, length):
    step = HALF_STEP * 2.0 * math.pi / BOX_LENGTH
    angles = components[:, None] * (jnp.arange(length // 2, dtype=jnp.float32) * step)[None, :]
    return jnp.cos(angles), jnp.sin(angles)


def mixing_matrix(orientations, weights):
    cosines = jnp.dot(orientations.T, orientations, precision=HIGHEST)
    previous = jnp.ones_like(cosines)
    current = cosines
    combined = previous * (1.0 / (4.0 * math.pi))
    for degree in range(1, LMAX + 1):
        if degree > 1:
            previous, current = (
                current,
                ((2 * degree - 1) * cosines * current - (degree - 1) * previous) / degree,
            )
        combined = (
            combined
            + math.exp(-DECAY_RATE * degree * (degree + 1))
            * (2 * degree + 1)
            / (4.0 * math.pi)
            * current
        )
    return combined * weights[None, :]


def halves(values):
    high = values.astype(jnp.bfloat16)
    return high, (values - high.astype(jnp.float32)).astype(jnp.bfloat16)


def wide_table(values):
    high = values.astype(jnp.bfloat16)
    low = (values - high.astype(np.float32)).astype(jnp.bfloat16)
    return np.concatenate([high, high, low], axis=1)


def wide_left(values):
    high, low = halves(values)
    return jnp.concatenate([high, high, low], axis=1)


def wide_right(values):
    high, low = halves(values)
    return jnp.concatenate([high, low, high], axis=0)


def product(left, right):
    return jnp.dot(left, right, preferred_element_type=jnp.float32)


def swap(values):
    return pltpu.roll(values, values.shape[1] // 2, 1)


def low_lanes(shape):
    return lax.broadcasted_iota(jnp.int32, shape, 1) < shape[1] // 2


def circulant(row):
    length = row.shape[1]
    return pltpu.roll(jnp.broadcast_to(row, (length, length)), 0, 1, stride=1, stride_axis=0)


def narrow_product(left, right):
    left_high, left_low = halves(left)
    high, low = halves(right)
    top = jnp.concatenate([high, low], axis=1)
    bottom = jnp.concatenate([high, jnp.zeros_like(low)], axis=1)
    both = product(
        jnp.concatenate([left_high, left_low], axis=1), jnp.concatenate([top, bottom], axis=0)
    )
    columns = right.shape[1]
    return both[:, :columns] + both[:, columns:]


def shift_rows(orientations, inverse):
    length = inverse.shape[0]
    half = length // 2
    components = jnp.concatenate([orientations[0:1], -orientations[1:2]], axis=1)
    orders = lax.broadcasted_iota(jnp.int32, (half, components.shape[1]), 0)
    angles = components * (orders.astype(jnp.float32) * (HALF_STEP * 2.0 * math.pi / BOX_LENGTH))
    sines = jnp.where(orders == 0, 1.0, jnp.sin(angles))
    waves = jnp.concatenate([jnp.cos(angles), sines], axis=0)
    columns = jnp.dot(inverse, waves, precision=HIGHEST, preferred_element_type=jnp.float32)
    return columns.T


def plane_kernel(count, start, propagator_ref, field_ref, orientations_ref, inverse_ref, out_ref, damping_ref, rows_ref):
    step = pl.program_id(0)
    batch = propagator_ref.shape[1]
    total = rows_ref.shape[0] // 2
    first_own = start()

    @pl.when(step == 0)
    def _():
        damping_ref[...] = jnp.exp(-0.5 * HALF_STEP * field_ref[...])
        rows_ref[...] = shift_rows(orientations_ref[...], inverse_ref[...])

    for n in range(batch):
        row = step * batch + n
        moved = []
        for part in range(2):
            own = first_own + part * count + row
            damped = propagator_ref[part, n] * damping_ref[...]
            shift_x = circulant(rows_ref[pl.ds(own, 1), :])
            shift_y = circulant(rows_ref[pl.ds(total + own, 1), :])
            moved.append(narrow_product(shift_y, narrow_product(damped, shift_x)))
        first, second = moved
        low = low_lanes(first.shape)
        rows = pl.ds(row, first.shape[0], stride=count)
        out_ref[0, rows, :] = jnp.where(low, first, swap(second))
        out_ref[1, rows, :] = jnp.where(low, swap(first), second)


def line_kernel(depth, lines_ref, forward_ref, inverse_ref, cos_ref, sin_ref, mixing_ref, out_ref, advected_ref):
    count = lines_ref.shape[1] // depth
    half = depth // 2
    lanes = lines_ref.shape[2]
    pairs = count // 2
    pitch = advected_ref.shape[0] // depth

    def shift(item, carry):
        group = item // pairs
        row = 2 * (item % pairs)
        taken = [lines_ref[group, pl.ds(row + n, depth, stride=count), :] for n in range(2)]
        spectrum = product(forward_ref[...], wide_right(jnp.concatenate(taken, axis=1)))
        cosines = jnp.concatenate([cos_ref[group, row + n] for n in range(2)], axis=1)
        sines = jnp.concatenate([sin_ref[group, row + n] for n in range(2)], axis=1)
        real, imaginary = spectrum[:half], spectrum[half:]
        turned = jnp.concatenate(
            [real * cosines - imaginary * sines, real * sines + imaginary * cosines], axis=0
        )
        advected = product(inverse_ref[...], wide_right(turned))
        for n in range(2):
            rows = pl.ds(group * count + row + n, depth, stride=pitch)
            advected_ref[rows, :] = advected[:, n * lanes : (n + 1) * lanes]
        return carry

    lax.fori_loop(0, 2 * pairs, shift, 0, unroll=2)
    both = 2 * count
    mixing = wide_left(mixing_ref[...])
    low = low_lanes((both, lanes))

    def mix(step, carry):
        stacked = []
        for n in range(2):
            base = (4 * step + 2 * n) * pitch
            first = advected_ref[pl.ds(base, both), :]
            second = advected_ref[pl.ds(base + pitch, both), :]
            stacked.append(
                jnp.concatenate(
                    [jnp.where(low, first, swap(second)), jnp.where(low, swap(first), second)], axis=0
                )
            )
        mixed = product(mixing, wide_right(jnp.concatenate(stacked, axis=1)))
        for n in range(2):
            place = mixed[:, n * lanes : (n + 1) * lanes]
            first, second = place[:both], place[both:]
            for m, values in enumerate(
                (jnp.where(low, first, swap(second)), jnp.where(low, swap(first), second))
            ):
                target = pl.ds((4 * step + 2 * n + m) * count, count)
                out_ref[0, target, :] = values[:count]
                out_ref[1, target, :] = values[count:]
        return carry

    lax.fori_loop(0, depth // 4, mix, 0, unroll=UNROLL)


def close_kernel(mixed_ref, field_ref, out_ref):
    depth = field_ref.shape[0]
    count = out_ref.shape[1]
    damping = jnp.exp(-0.5 * HALF_STEP * field_ref[...])
    low = low_lanes(damping.shape)
    for row in range(count):
        first = mixed_ref[0, pl.ds(row, depth, stride=count), :]
        second = mixed_ref[1, pl.ds(row, depth, stride=count), :]
        out_ref[0, row] = jnp.where(low, first, swap(second)) * damping
        out_ref[1, row] = jnp.where(low, swap(first), second) * damping


def whole(shape):
    return pl.BlockSpec(shape, lambda row: (0,) * len(shape))


def local(propagator, field, orientations, weights):
    own, depth, rows, cols = propagator.shape
    groups = lax.axis_size("orient")
    slabs = lax.axis_size("slab")
    total_z = depth * slabs
    count = own // 2
    half = total_z // 2
    plane = field[0]
    message = (groups, slabs * count, cols)
    forward, inverse = packed_tables(total_z)
    batch = 2
    sent = pl.pallas_call(
        functools.partial(plane_kernel, count, lambda: lax.axis_index("orient") * own),
        grid=(count // batch,),
        in_specs=[
            pl.BlockSpec((2, batch, rows, cols), lambda row: (0, row, 0, 0)),
            whole((rows, cols)),
            whole(orientations.shape),
            whole((cols, cols)),
        ],
        out_specs=whole(message),
        out_shape=jax.ShapeDtypeStruct(message, jnp.float32),
        scratch_shapes=[
            pltpu.VMEM((rows, cols), jnp.float32),
            pltpu.VMEM((2 * groups * own, cols), jnp.float32),
        ],
        compiler_params=PARAMS,
        name="plane",
    )(propagator.reshape(2, count, rows, cols), plane, orientations, packed_tables(cols)[1])

    lines = lax.all_to_all(sent.reshape(groups * slabs, count, cols), AXES, 0, 0, tiled=True)

    cosines, sines = phase_tables(orientations[2], total_z)

    def by_lane(table):
        table = table.reshape(groups, 2, count, half).transpose(0, 2, 3, 1)
        return jnp.repeat(table, cols // 2, axis=3)

    matrix = mixing_matrix(orientations, weights)
    matrix = matrix.reshape(groups, 2, count, groups, 2, count).transpose(1, 0, 2, 4, 3, 5)
    matrix = matrix.reshape(2 * own, 2 * own)
    back = pl.pallas_call(
        functools.partial(line_kernel, total_z),
        out_shape=jax.ShapeDtypeStruct(message, jnp.float32),
        scratch_shapes=[pltpu.VMEM((total_z * (groups * count + 8), cols), jnp.float32)],
        compiler_params=PARAMS,
        name="line",
    )(
        lines.reshape(message),
        wide_table(forward.T),
        wide_table(inverse),
        by_lane(cosines),
        by_lane(sines),
        matrix,
    )
    mixed = lax.all_to_all(back.reshape(groups * slabs, count, cols), AXES, 0, 0, tiled=True)
    strip = rows // 4
    result = pl.pallas_call(
        close_kernel,
        grid=(rows // strip,),
        in_specs=[
            pl.BlockSpec((groups, strip * count, cols), lambda step: (0, step, 0)),
            pl.BlockSpec((strip, cols), lambda step: (step, 0)),
        ],
        out_specs=pl.BlockSpec((2, count, strip, cols), lambda step: (0, 0, step, 0)),
        out_shape=jax.ShapeDtypeStruct((2, count, rows, cols), jnp.float32),
        compiler_params=PARAMS,
        name="close",
    )(mixed.reshape(message), plane)
    return result.reshape(own, 1, rows, cols)


def solution(mesh):
    in_specs = (P("orient", "slab", None, None), P("slab", None, None), P(), P())
    out_specs = P("orient", "slab", None, None)
    return jax.shard_map(local, mesh=mesh, in_specs=in_specs, out_specs=out_specs, check_vma=False)
```

```python
import functools
import math

import jax
import jax.numpy as jnp
import numpy as np
from jax import lax
from jax.experimental import pallas as pl
from jax.experimental.pallas import tpu as pltpu
from jax.sharding import PartitionSpec as P

LMAX = 10


HALF_STEP = 0.1
BOX_LENGTH = 12.8
DECAY_RATE = 0.01
HIGHEST = lax.Precision.HIGHEST
AXES = ("orient", "slab")
SMALL = pltpu.CompilerParams(vmem_limit_bytes=16 * 1024 * 1024)
LARGE = pltpu.CompilerParams()
BATCH = 8
SHIFT_UNROLL = 8
MIX_UNROLL = 16


def packed_tables(length):
    half = length // 2
    positions = np.arange(length)
    orders = np.arange(half)
    angles = (positions[:, None] * orders[None, :] % length) * (2.0 * math.pi / length)
    nyquist = np.where(positions % 2 == 0, 1.0, -1.0)
    sines = np.where(orders[None, :] == 0, nyquist[:, None], np.sin(angles))
    forward = np.concatenate([np.cos(angles), sines], axis=1)
    scale = np.where(np.arange(length) % half == 0, 1.0, 2.0) / length
    return forward.astype(np.float32), (forward * scale[None, :]).astype(np.float32)


def mixing_matrix(orientations, weights):
    cosines = jnp.dot(orientations.T, orientations, precision=HIGHEST)
    previous = jnp.ones_like(cosines)
    current = cosines
    combined = previous * (1.0 / (4.0 * math.pi))
    for degree in range(1, LMAX + 1):
        if degree > 1:
            previous, current = (
                current,
                ((2 * degree - 1) * cosines * current - (degree - 1) * previous) / degree,
            )
        combined = (
            combined
            + math.exp(-DECAY_RATE * degree * (degree + 1))
            * (2 * degree + 1)
            / (4.0 * math.pi)
            * current
        )
    return combined * weights[None, :]


def halves(values):
    high = values.astype(jnp.bfloat16)
    return high, (values - high.astype(jnp.float32)).astype(jnp.bfloat16)


def wide_table(values):
    high = values.astype(jnp.bfloat16)
    low = (values - high.astype(np.float32)).astype(jnp.bfloat16)
    return np.concatenate([high, high, low], axis=1)


def wide_left(values):
    high, low = halves(values)
    return jnp.concatenate([high, high, low], axis=1)


def wide_right(values):
    high, low = halves(values)
    return jnp.concatenate([high, low, high], axis=0)


def product(left, right):
    return jnp.dot(left, right, preferred_element_type=jnp.float32)


def swap(values):
    return pltpu.roll(values, values.shape[1] // 2, 1)


def low_lanes(shape):
    return lax.broadcasted_iota(jnp.int32, shape, 1) < shape[1] // 2


def circulant(row):
    length = row.shape[1]
    return pltpu.roll(jnp.broadcast_to(row, (length, length)), 0, 1, stride=1, stride_axis=0)


def narrow_product(left, right):
    left_high, left_low = halves(left)
    high, low = halves(right)
    top = jnp.concatenate([high, low], axis=1)
    bottom = jnp.concatenate([high, jnp.zeros_like(low)], axis=1)
    both = product(
        jnp.concatenate([left_high, left_low], axis=1), jnp.concatenate([top, bottom], axis=0)
    )
    columns = right.shape[1]
    return both[:, :columns] + both[:, columns:]


def shift_rows(orientations, inverse):
    length = inverse.shape[0]
    half = length // 2
    components = jnp.concatenate([orientations[0:1], -orientations[1:2]], axis=1)
    orders = lax.broadcasted_iota(jnp.int32, (half, components.shape[1]), 0)
    angles = components * (orders.astype(jnp.float32) * (HALF_STEP * 2.0 * math.pi / BOX_LENGTH))
    sines = jnp.where(orders == 0, 1.0, jnp.sin(angles))
    waves = jnp.concatenate([jnp.cos(angles), sines], axis=0)
    columns = jnp.dot(inverse, waves, precision=HIGHEST, preferred_element_type=jnp.float32)
    return columns.T


def plane_kernel(count, start, propagator_ref, field_ref, orientations_ref, inverse_ref, out_ref, damping_ref, rows_ref):
    step = pl.program_id(0)
    batch = propagator_ref.shape[1]
    total = rows_ref.shape[0] // 2
    first_own = start()

    @pl.when(step == 0)
    def _():
        damping_ref[...] = jnp.exp(-0.5 * HALF_STEP * field_ref[...])
        rows_ref[...] = shift_rows(orientations_ref[...], inverse_ref[...])

    for n in range(batch):
        row = step * batch + n
        moved = []
        for part in range(2):
            own = first_own + part * count + row
            damped = propagator_ref[part, n] * damping_ref[...]
            shift_x = circulant(rows_ref[pl.ds(own, 1), :])
            shift_y = circulant(rows_ref[pl.ds(total + own, 1), :])
            moved.append(narrow_product(shift_y, narrow_product(damped, shift_x)))
        first, second = moved
        low = low_lanes(first.shape)
        rows = pl.ds(row, first.shape[0], stride=count)
        out_ref[0, rows, :] = jnp.where(low, first, swap(second))
        out_ref[1, rows, :] = jnp.where(low, swap(first), second)


def line_kernel(depth, lines_ref, forward_ref, inverse_ref, cos_ref, sin_ref, mixing_ref, out_ref, advected_ref):
    count = lines_ref.shape[1] // depth
    half = depth // 2
    lanes = lines_ref.shape[2]
    pairs = count // 2
    pitch = advected_ref.shape[0] // depth

    def shift(item, carry):
        group = item // pairs
        row = 2 * (item % pairs)
        taken = [lines_ref[group, pl.ds(row + n, depth, stride=count), :] for n in range(2)]
        spectrum = product(forward_ref[...], wide_right(jnp.concatenate(taken, axis=1)))
        cosines = jnp.concatenate([cos_ref[group, row + n] for n in range(2)], axis=1)
        sines = jnp.concatenate([sin_ref[group, row + n] for n in range(2)], axis=1)
        real, imaginary = spectrum[:half], spectrum[half:]
        turned = jnp.concatenate(
            [real * cosines - imaginary * sines, real * sines + imaginary * cosines], axis=0
        )
        advected = product(inverse_ref[...], wide_right(turned))
        for n in range(2):
            rows = pl.ds(group * count + row + n, depth, stride=pitch)
            advected_ref[rows, :] = advected[:, n * lanes : (n + 1) * lanes]
        return carry

    lax.fori_loop(0, 2 * pairs, shift, 0, unroll=SHIFT_UNROLL)
    both = 2 * count
    mixing = wide_left(mixing_ref[...])
    low = low_lanes((both, lanes))

    def mix(step, carry):
        stacked = []
        for n in range(2):
            base = (4 * step + 2 * n) * pitch
            first = advected_ref[pl.ds(base, both), :]
            second = advected_ref[pl.ds(base + pitch, both), :]
            stacked.append(
                jnp.concatenate(
                    [jnp.where(low, first, swap(second)), jnp.where(low, swap(first), second)], axis=0
                )
            )
        mixed = product(mixing, wide_right(jnp.concatenate(stacked, axis=1)))
        for n in range(2):
            place = mixed[:, n * lanes : (n + 1) * lanes]
            first, second = place[:both], place[both:]
            for m, values in enumerate(
                (jnp.where(low, first, swap(second)), jnp.where(low, swap(first), second))
            ):
                target = pl.ds((4 * step + 2 * n + m) * count, count)
                out_ref[0, target, :] = values[:count]
                out_ref[1, target, :] = values[count:]
        return carry

    lax.fori_loop(0, depth // 4, mix, 0, unroll=MIX_UNROLL)


def phase_kernel(orientations_ref, cos_ref, sin_ref):
    groups, count, half, lanes = cos_ref.shape
    component = orientations_ref[2:3, :]
    orders = lax.broadcasted_iota(jnp.int32, (half, component.shape[1]), 0)
    angles = component * (orders.astype(jnp.float32) * (HALF_STEP * 2.0 * math.pi / BOX_LENGTH))
    low = low_lanes((half, lanes))
    for table, out_ref in ((jnp.cos(angles), cos_ref), (jnp.sin(angles), sin_ref)):
        for group in range(groups):
            for row in range(count):
                first = 2 * count * group + row
                second = first + count
                out_ref[group, row] = jnp.where(
                    low,
                    jnp.broadcast_to(table[:, first : first + 1], (half, lanes)),
                    jnp.broadcast_to(table[:, second : second + 1], (half, lanes)),
                )


def close_kernel(mixed_ref, field_ref, out_ref):
    depth = field_ref.shape[0]
    count = out_ref.shape[1]
    damping = jnp.exp(-0.5 * HALF_STEP * field_ref[...])
    low = low_lanes(damping.shape)
    for row in range(count):
        first = mixed_ref[0, pl.ds(row, depth, stride=count), :]
        second = mixed_ref[1, pl.ds(row, depth, stride=count), :]
        out_ref[0, row] = jnp.where(low, first, swap(second)) * damping
        out_ref[1, row] = jnp.where(low, swap(first), second) * damping


def whole(shape):
    return pl.BlockSpec(shape, lambda row: (0,) * len(shape))


def run_plane(propagator, plane, orientations, start):
    _, count, rows, cols = propagator.shape
    message = (2, rows * count, cols)
    return pl.pallas_call(
        functools.partial(plane_kernel, count, start),
        grid=(count // BATCH,),
        in_specs=[
            pl.BlockSpec((2, BATCH, rows, cols), lambda row: (0, row, 0, 0)),
            whole((rows, cols)),
            whole(orientations.shape),
            whole((cols, cols)),
        ],
        out_specs=whole(message),
        out_shape=jax.ShapeDtypeStruct(message, jnp.float32),
        scratch_shapes=[
            pltpu.VMEM((rows, cols), jnp.float32),
            pltpu.VMEM((2 * orientations.shape[1], cols), jnp.float32),
        ],
        compiler_params=LARGE,
        name="plane",
    )(propagator, plane, orientations, packed_tables(cols)[1])


def run_phase(orientations, groups, count, half, lanes):
    shape = jax.ShapeDtypeStruct((groups, count, half, lanes), jnp.float32)
    return pl.pallas_call(
        phase_kernel, out_shape=(shape, shape), compiler_params=SMALL, name="phase"
    )(orientations)


def run_line(lines, cosines, sines, matrix, total_z):
    groups, height, cols = lines.shape
    forward, inverse = packed_tables(total_z)
    pitch = groups * (height // total_z) + 8
    return pl.pallas_call(
        functools.partial(line_kernel, total_z),
        out_shape=jax.ShapeDtypeStruct(lines.shape, jnp.float32),
        scratch_shapes=[pltpu.VMEM((total_z * pitch, cols), jnp.float32)],
        compiler_params=SMALL,
        name="line",
    )(lines, wide_table(forward.T), wide_table(inverse), cosines, sines, matrix)


def run_close(mixed, plane, count):
    groups = mixed.shape[0]
    rows, cols = plane.shape
    strip = rows // 4
    return pl.pallas_call(
        close_kernel,
        grid=(rows // strip,),
        in_specs=[
            pl.BlockSpec((groups, strip * count, cols), lambda step: (0, step, 0)),
            pl.BlockSpec((strip, cols), lambda step: (step, 0)),
        ],
        out_specs=pl.BlockSpec((2, count, strip, cols), lambda step: (0, 0, step, 0)),
        out_shape=jax.ShapeDtypeStruct((2, count, rows, cols), jnp.float32),
        compiler_params=SMALL,
        name="close",
    )(mixed, plane)


def local(propagator, field, orientations, weights):
    own, depth, rows, cols = propagator.shape
    groups = lax.axis_size("orient")
    slabs = lax.axis_size("slab")
    total_z = depth * slabs
    count = own // 2
    plane = field[0]
    sent = run_plane(
        propagator.reshape(2, count, rows, cols), plane, orientations, lambda: lax.axis_index("orient") * own
    )
    lines = lax.all_to_all(sent.reshape(groups * slabs, count, cols), AXES, 0, 0, tiled=True)
    cosines, sines = run_phase(orientations, groups, count, total_z // 2, cols)
    matrix = mixing_matrix(orientations, weights)
    matrix = matrix.reshape(groups, 2, count, groups, 2, count).transpose(1, 0, 2, 4, 3, 5)
    matrix = matrix.reshape(2 * own, 2 * own)
    back = run_line(lines.reshape(sent.shape), cosines, sines, matrix, total_z)
    mixed = lax.all_to_all(back.reshape(groups * slabs, count, cols), AXES, 0, 0, tiled=True)
    result = run_close(mixed.reshape(sent.shape), plane, count)
    return result.reshape(own, 1, rows, cols)


def solution(mesh):
    in_specs = (P("orient", "slab", None, None), P("slab", None, None), P(), P())
    out_specs = P("orient", "slab", None, None)
    return jax.shard_map(local, mesh=mesh, in_specs=in_specs, out_specs=out_specs, check_vma=False)
```

```python
import functools
import math

import jax
import jax.numpy as jnp
import numpy as np
from jax import lax
from jax.experimental import pallas as pl
from jax.experimental.pallas import tpu as pltpu
from jax.sharding import PartitionSpec as P

LMAX = 10


HALF_STEP = 0.1
BOX_LENGTH = 12.8
DECAY_RATE = 0.01
HIGHEST = lax.Precision.HIGHEST
AXES = ("orient", "slab")
SMALL = pltpu.CompilerParams(vmem_limit_bytes=16 * 1024 * 1024)
LARGE = pltpu.CompilerParams()
BATCH = 8
STRIPS = 2
MIX_UNROLL = 32


def packed_tables(length):
    half = length // 2
    positions = np.arange(length)
    orders = np.arange(half)
    angles = (positions[:, None] * orders[None, :] % length) * (2.0 * math.pi / length)
    nyquist = np.where(positions % 2 == 0, 1.0, -1.0)
    sines = np.where(orders[None, :] == 0, nyquist[:, None], np.sin(angles))
    forward = np.concatenate([np.cos(angles), sines], axis=1)
    scale = np.where(np.arange(length) % half == 0, 1.0, 2.0) / length
    return forward.astype(np.float32), (forward * scale[None, :]).astype(np.float32)


def mixing_matrix(orientations, weights):
    cosines = jnp.dot(orientations.T, orientations, precision=HIGHEST)
    previous = jnp.ones_like(cosines)
    current = cosines
    combined = previous * (1.0 / (4.0 * math.pi))
    for degree in range(1, LMAX + 1):
        if degree > 1:
            previous, current = (
                current,
                ((2 * degree - 1) * cosines * current - (degree - 1) * previous) / degree,
            )
        combined = (
            combined
            + math.exp(-DECAY_RATE * degree * (degree + 1))
            * (2 * degree + 1)
            / (4.0 * math.pi)
            * current
        )
    return combined * weights[None, :]


def halves(values):
    high = values.astype(jnp.bfloat16)
    return high, (values - high.astype(jnp.float32)).astype(jnp.bfloat16)


def wide_table(values):
    high = values.astype(jnp.bfloat16)
    low = (values - high.astype(np.float32)).astype(jnp.bfloat16)
    return np.concatenate([high, high, low], axis=1)


def wide_left(values):
    high, low = halves(values)
    return jnp.concatenate([high, high, low], axis=1)


def wide_right(values):
    high, low = halves(values)
    return jnp.concatenate([high, low, high], axis=0)


def product(left, right):
    return jnp.dot(left, right, preferred_element_type=jnp.float32)


def swap(values):
    return pltpu.roll(values, values.shape[1] // 2, 1)


def low_lanes(shape):
    return lax.broadcasted_iota(jnp.int32, shape, 1) < shape[1] // 2


def circulant(row):
    length = row.shape[1]
    return pltpu.roll(jnp.broadcast_to(row, (length, length)), 0, 1, stride=1, stride_axis=0)


def narrow_product(left, right):
    left_high, left_low = halves(left)
    high, low = halves(right)
    top = jnp.concatenate([high, low], axis=1)
    bottom = jnp.concatenate([high, jnp.zeros_like(low)], axis=1)
    both = product(
        jnp.concatenate([left_high, left_low], axis=1), jnp.concatenate([top, bottom], axis=0)
    )
    columns = right.shape[1]
    return both[:, :columns] + both[:, columns:]


def shift_rows(orientations, inverse):
    length = inverse.shape[0]
    half = length // 2
    components = jnp.concatenate([orientations[0:1], -orientations[1:2]], axis=1)
    orders = lax.broadcasted_iota(jnp.int32, (half, components.shape[1]), 0)
    angles = components * (orders.astype(jnp.float32) * (HALF_STEP * 2.0 * math.pi / BOX_LENGTH))
    sines = jnp.where(orders == 0, 1.0, jnp.sin(angles))
    waves = jnp.concatenate([jnp.cos(angles), sines], axis=0)
    columns = jnp.dot(inverse, waves, precision=HIGHEST, preferred_element_type=jnp.float32)
    return columns.T


def plane_kernel(count, start, propagator_ref, field_ref, orientations_ref, inverse_ref, out_ref, damping_ref, rows_ref):
    step = pl.program_id(0)
    batch = propagator_ref.shape[1]
    total = rows_ref.shape[0] // 2
    first_own = start()

    @pl.when(step == 0)
    def _():
        damping_ref[...] = jnp.exp(-0.5 * HALF_STEP * field_ref[...])
        rows_ref[...] = shift_rows(orientations_ref[...], inverse_ref[...])

    for n in range(batch):
        row = step * batch + n
        moved = []
        for part in range(2):
            own = first_own + part * count + row
            damped = propagator_ref[part, n] * damping_ref[...]
            shift_x = circulant(rows_ref[pl.ds(own, 1), :])
            shift_y = circulant(rows_ref[pl.ds(total + own, 1), :])
            moved.append(narrow_product(shift_y, narrow_product(damped, shift_x)))
        first, second = moved
        low = low_lanes(first.shape)
        rows = pl.ds(row, first.shape[0], stride=count)
        out_ref[0, rows, :] = jnp.where(low, first, swap(second))
        out_ref[1, rows, :] = jnp.where(low, swap(first), second)


def line_kernel(depth, lines_ref, forward_ref, inverse_ref, phases_ref, mixing_ref, out_ref, advected_ref):
    groups = lines_ref.shape[0]
    count = lines_ref.shape[1] // depth
    half = depth // 2
    lanes = lines_ref.shape[2]
    pitch = advected_ref.shape[0] // depth
    quarter = lanes // 4
    even = (lax.broadcasted_iota(jnp.int32, (half, lanes), 1) // quarter) % 2 == 0

    def spread(group, row):
        packed = phases_ref[group, row]
        return (
            jnp.where(even, packed, pltpu.roll(packed, quarter, 1)),
            jnp.where(even, pltpu.roll(packed, lanes - quarter, 1), packed),
        )

    for group in range(groups):
        for row in range(0, count, 2):
            taken = [lines_ref[group, pl.ds(row + n, depth, stride=count), :] for n in range(2)]
            spectrum = product(forward_ref[...], wide_right(jnp.concatenate(taken, axis=1)))
            cosines, sines = (
                jnp.concatenate(tables, axis=1) for tables in zip(*(spread(group, row + n) for n in range(2)))
            )
            real, imaginary = spectrum[:half], spectrum[half:]
            turned = jnp.concatenate(
                [real * cosines - imaginary * sines, real * sines + imaginary * cosines], axis=0
            )
            advected = product(inverse_ref[...], wide_right(turned))
            for n in range(2):
                rows = pl.ds(group * count + row + n, depth, stride=pitch)
                advected_ref[rows, :] = advected[:, n * lanes : (n + 1) * lanes]

    both = 2 * count
    mixing = wide_left(mixing_ref[...])
    low = low_lanes((both, lanes))

    def mix(step, carry):
        stacked = []
        for n in range(2):
            base = (4 * step + 2 * n) * pitch
            first = advected_ref[pl.ds(base, both), :]
            second = advected_ref[pl.ds(base + pitch, both), :]
            stacked.append(
                jnp.concatenate(
                    [jnp.where(low, first, swap(second)), jnp.where(low, swap(first), second)], axis=0
                )
            )
        mixed = product(mixing, wide_right(jnp.concatenate(stacked, axis=1)))
        for n in range(2):
            place = mixed[:, n * lanes : (n + 1) * lanes]
            first, second = place[:both], place[both:]
            for m, values in enumerate(
                (jnp.where(low, first, swap(second)), jnp.where(low, swap(first), second))
            ):
                target = pl.ds((4 * step + 2 * n + m) * count, count)
                out_ref[0, target, :] = values[:count]
                out_ref[1, target, :] = values[count:]
        return carry

    lax.fori_loop(0, depth // 4, mix, 0, unroll=MIX_UNROLL)


def phase_kernel(orientations_ref, out_ref):
    groups, count, half, lanes = out_ref.shape
    component = orientations_ref[2:3, :]
    orders = lax.broadcasted_iota(jnp.int32, (half, component.shape[1]), 0)
    angles = component * (orders.astype(jnp.float32) * (HALF_STEP * 2.0 * math.pi / BOX_LENGTH))
    cosines, sines = jnp.cos(angles), jnp.sin(angles)
    quarters = lax.broadcasted_iota(jnp.int32, (half, lanes), 1) // (lanes // 4)
    for group in range(groups):
        for row in range(count):
            first = 2 * count * group + row
            values = [
                jnp.broadcast_to(table[:, n : n + 1], (half, lanes))
                for n in (first, first + count)
                for table in (cosines, sines)
            ]
            low = jnp.where(quarters == 0, values[0], values[1])
            high = jnp.where(quarters == 2, values[2], values[3])
            out_ref[group, row] = jnp.where(quarters < 2, low, high)


def close_kernel(mixed_ref, field_ref, out_ref):
    depth = out_ref.shape[2]
    count = out_ref.shape[1]
    base = pl.program_id(0) * depth
    damping = jnp.exp(-0.5 * HALF_STEP * field_ref[pl.ds(base, depth), :])
    low = low_lanes(damping.shape)
    for row in range(count):
        rows = pl.ds(base * count + row, depth, stride=count)
        first = mixed_ref[0, rows, :]
        second = mixed_ref[1, rows, :]
        out_ref[0, row] = jnp.where(low, first, swap(second)) * damping
        out_ref[1, row] = jnp.where(low, swap(first), second) * damping


def whole(shape):
    return pl.BlockSpec(shape, lambda row: (0,) * len(shape))


def run_plane(propagator, plane, orientations, start):
    _, count, rows, cols = propagator.shape
    message = (2, rows * count, cols)
    return pl.pallas_call(
        functools.partial(plane_kernel, count, start),
        grid=(count // BATCH,),
        in_specs=[
            pl.BlockSpec((2, BATCH, rows, cols), lambda row: (0, row, 0, 0)),
            whole((rows, cols)),
            whole(orientations.shape),
            whole((cols, cols)),
        ],
        out_specs=whole(message),
        out_shape=jax.ShapeDtypeStruct(message, jnp.float32),
        scratch_shapes=[
            pltpu.VMEM((rows, cols), jnp.float32),
            pltpu.VMEM((2 * orientations.shape[1], cols), jnp.float32),
        ],
        compiler_params=LARGE,
        name="plane",
    )(propagator, plane, orientations, packed_tables(cols)[1])


def run_phase(orientations, groups, count, half, lanes):
    shape = jax.ShapeDtypeStruct((groups, count, half, lanes), jnp.float32)
    return pl.pallas_call(
        phase_kernel, out_shape=shape, compiler_params=SMALL, name="phase"
    )(orientations)


def run_line(lines, phases, matrix, total_z):
    groups, height, cols = lines.shape
    forward, inverse = packed_tables(total_z)
    pitch = groups * (height // total_z) + 8
    return pl.pallas_call(
        functools.partial(line_kernel, total_z),
        out_shape=jax.ShapeDtypeStruct(lines.shape, jnp.float32),
        scratch_shapes=[pltpu.VMEM((total_z * pitch, cols), jnp.float32)],
        compiler_params=SMALL,
        name="line",
    )(lines, wide_table(forward.T), wide_table(inverse), phases, matrix)


def run_close(mixed, plane, count):
    rows, cols = plane.shape
    strip = rows // STRIPS
    return pl.pallas_call(
        close_kernel,
        grid=(rows // strip,),
        in_specs=[pl.BlockSpec(memory_space=pltpu.VMEM)] * 2,
        out_specs=pl.BlockSpec((2, count, strip, cols), lambda step: (0, 0, step, 0)),
        out_shape=jax.ShapeDtypeStruct((2, count, rows, cols), jnp.float32),
        compiler_params=SMALL,
        name="close",
    )(mixed, plane)


def local(propagator, field, orientations, weights):
    own, depth, rows, cols = propagator.shape
    groups = lax.axis_size("orient")
    slabs = lax.axis_size("slab")
    total_z = depth * slabs
    count = own // 2
    plane = field[0]
    sent = run_plane(
        propagator.reshape(2, count, rows, cols), plane, orientations, lambda: lax.axis_index("orient") * own
    )
    lines = lax.all_to_all(sent.reshape(groups * slabs, count, cols), AXES, 0, 0, tiled=True)
    phases = run_phase(orientations, groups, count, total_z // 2, cols)
    matrix = mixing_matrix(orientations, weights)
    matrix = matrix.reshape(groups, 2, count, groups, 2, count).transpose(1, 0, 2, 4, 3, 5)
    matrix = matrix.reshape(2 * own, 2 * own)
    back = run_line(lines.reshape(sent.shape), phases, matrix, total_z)
    mixed = lax.all_to_all(back.reshape(groups * slabs, count, cols), AXES, 0, 0, tiled=True)
    result = run_close(mixed.reshape(sent.shape), plane, count)
    return result.reshape(own, 1, rows, cols)


def solution(mesh):
    in_specs = (P("orient", "slab", None, None), P("slab", None, None), P(), P())
    out_specs = P("orient", "slab", None, None)
    return jax.shard_map(local, mesh=mesh, in_specs=in_specs, out_specs=out_specs, check_vma=False)
```

```python
import functools
import math

import jax
import jax.numpy as jnp
import numpy as np
from jax import lax
from jax.experimental import pallas as pl
from jax.experimental.pallas import tpu as pltpu
from jax.sharding import PartitionSpec as P

LMAX = 10


HALF_STEP = 0.1
BOX_LENGTH = 12.8
DECAY_RATE = 0.01
HIGHEST = lax.Precision.HIGHEST
AXES = ("orient", "slab")
SMALL = pltpu.CompilerParams(vmem_limit_bytes=16 * 1024 * 1024)
LARGE = pltpu.CompilerParams()
BATCH = 8
STRIPS = 8
MIX_UNROLL = 32


def packed_tables(length):
    half = length // 2
    positions = np.arange(length)
    orders = np.arange(half)
    angles = (positions[:, None] * orders[None, :] % length) * (2.0 * math.pi / length)
    nyquist = np.where(positions % 2 == 0, 1.0, -1.0)
    sines = np.where(orders[None, :] == 0, nyquist[:, None], np.sin(angles))
    forward = np.concatenate([np.cos(angles), sines], axis=1)
    scale = np.where(np.arange(length) % half == 0, 1.0, 2.0) / length
    return forward.astype(np.float32), (forward * scale[None, :]).astype(np.float32)


def mixing_matrix(orientations, weights):
    cosines = jnp.dot(orientations.T, orientations, precision=HIGHEST)
    previous = jnp.ones_like(cosines)
    current = cosines
    combined = previous * (1.0 / (4.0 * math.pi))
    for degree in range(1, LMAX + 1):
        if degree > 1:
            previous, current = (
                current,
                ((2 * degree - 1) * cosines * current - (degree - 1) * previous) / degree,
            )
        combined = (
            combined
            + math.exp(-DECAY_RATE * degree * (degree + 1))
            * (2 * degree + 1)
            / (4.0 * math.pi)
            * current
        )
    return combined * weights[None, :]


def halves(values):
    high = values.astype(jnp.bfloat16)
    return high, (values - high.astype(jnp.float32)).astype(jnp.bfloat16)


def wide_table(values):
    high = values.astype(jnp.bfloat16)
    low = (values - high.astype(np.float32)).astype(jnp.bfloat16)
    return np.concatenate([high, high, low], axis=1)


def wide_left(values):
    high, low = halves(values)
    return jnp.concatenate([high, high, low], axis=1)


def wide_right(values):
    high, low = halves(values)
    return jnp.concatenate([high, low, high], axis=0)


def product(left, right):
    return jnp.dot(left, right, preferred_element_type=jnp.float32)


def swap(values):
    return pltpu.roll(values, values.shape[1] // 2, 1)


def low_lanes(shape):
    return lax.broadcasted_iota(jnp.int32, shape, 1) < shape[1] // 2


def circulant(row):
    length = row.shape[1]
    return pltpu.roll(jnp.broadcast_to(row, (length, length)), 0, 1, stride=1, stride_axis=0)


def narrow_product(left, right):
    left_high, left_low = halves(left)
    high, low = halves(right)
    top = jnp.concatenate([high, low], axis=1)
    bottom = jnp.concatenate([high, jnp.zeros_like(low)], axis=1)
    both = product(
        jnp.concatenate([left_high, left_low], axis=1), jnp.concatenate([top, bottom], axis=0)
    )
    columns = right.shape[1]
    return both[:, :columns] + both[:, columns:]


def shift_rows(orientations, inverse):
    length = inverse.shape[0]
    half = length // 2
    components = jnp.concatenate([orientations[0:1], -orientations[1:2]], axis=1)
    orders = lax.broadcasted_iota(jnp.int32, (half, components.shape[1]), 0)
    angles = components * (orders.astype(jnp.float32) * (HALF_STEP * 2.0 * math.pi / BOX_LENGTH))
    sines = jnp.where(orders == 0, 1.0, jnp.sin(angles))
    waves = jnp.concatenate([jnp.cos(angles), sines], axis=0)
    columns = jnp.dot(inverse, waves, precision=HIGHEST, preferred_element_type=jnp.float32)
    return columns.T


def plane_kernel(count, start, propagator_ref, field_ref, orientations_ref, inverse_ref, out_ref, damping_ref, rows_ref):
    step = pl.program_id(0)
    batch = propagator_ref.shape[1]
    total = rows_ref.shape[0] // 2
    first_own = start()

    @pl.when(step == 0)
    def _():
        damping_ref[...] = jnp.exp(-0.5 * HALF_STEP * field_ref[...])
        rows_ref[...] = shift_rows(orientations_ref[...], inverse_ref[...])

    for n in range(batch):
        row = step * batch + n
        moved = []
        for part in range(2):
            own = first_own + part * count + row
            damped = propagator_ref[part, n] * damping_ref[...]
            shift_x = circulant(rows_ref[pl.ds(own, 1), :])
            shift_y = circulant(rows_ref[pl.ds(total + own, 1), :])
            moved.append(narrow_product(shift_y, narrow_product(damped, shift_x)))
        first, second = moved
        low = low_lanes(first.shape)
        out_ref[0, :, n, :] = jnp.where(low, first, swap(second))
        out_ref[1, :, n, :] = jnp.where(low, swap(first), second)


def line_kernel(depth, lines_ref, forward_ref, inverse_ref, phases_ref, mixing_ref, out_ref, advected_ref):
    groups = lines_ref.shape[0]
    count = lines_ref.shape[1] // depth
    half = depth // 2
    lanes = lines_ref.shape[2]
    pitch = advected_ref.shape[0] // depth
    quarter = lanes // 4
    even = (lax.broadcasted_iota(jnp.int32, (half, lanes), 1) // quarter) % 2 == 0

    def spread(group, row):
        packed = phases_ref[group, row]
        return (
            jnp.where(even, packed, pltpu.roll(packed, quarter, 1)),
            jnp.where(even, pltpu.roll(packed, lanes - quarter, 1), packed),
        )

    for group in range(groups):
        for row in range(0, count, 2):
            taken = [lines_ref[group, pl.ds(row + n, depth, stride=count), :] for n in range(2)]
            spectrum = product(forward_ref[...], wide_right(jnp.concatenate(taken, axis=1)))
            cosines, sines = (
                jnp.concatenate(tables, axis=1) for tables in zip(*(spread(group, row + n) for n in range(2)))
            )
            real, imaginary = spectrum[:half], spectrum[half:]
            turned = jnp.concatenate(
                [real * cosines - imaginary * sines, real * sines + imaginary * cosines], axis=0
            )
            advected = product(inverse_ref[...], wide_right(turned))
            for n in range(2):
                rows = pl.ds(group * count + row + n, depth, stride=pitch)
                advected_ref[rows, :] = advected[:, n * lanes : (n + 1) * lanes]

    both = 2 * count
    mixing = wide_left(mixing_ref[...])
    low = low_lanes((both, lanes))

    def mix(step, carry):
        stacked = []
        for n in range(2):
            base = (4 * step + 2 * n) * pitch
            first = advected_ref[pl.ds(base, both), :]
            second = advected_ref[pl.ds(base + pitch, both), :]
            stacked.append(
                jnp.concatenate(
                    [jnp.where(low, first, swap(second)), jnp.where(low, swap(first), second)], axis=0
                )
            )
        mixed = product(mixing, wide_right(jnp.concatenate(stacked, axis=1)))
        for n in range(2):
            place = mixed[:, n * lanes : (n + 1) * lanes]
            first, second = place[:both], place[both:]
            for m, values in enumerate(
                (jnp.where(low, first, swap(second)), jnp.where(low, swap(first), second))
            ):
                target = pl.ds((4 * step + 2 * n + m) * count, count)
                out_ref[0, target, :] = values[:count]
                out_ref[1, target, :] = values[count:]
        return carry

    lax.fori_loop(0, depth // 4, mix, 0, unroll=MIX_UNROLL)


def phase_kernel(orientations_ref, out_ref):
    groups, count, half, lanes = out_ref.shape
    component = orientations_ref[2:3, :]
    orders = lax.broadcasted_iota(jnp.int32, (half, component.shape[1]), 0)
    angles = component * (orders.astype(jnp.float32) * (HALF_STEP * 2.0 * math.pi / BOX_LENGTH))
    cosines, sines = jnp.cos(angles), jnp.sin(angles)
    quarters = lax.broadcasted_iota(jnp.int32, (half, lanes), 1) // (lanes // 4)
    for group in range(groups):
        for row in range(count):
            first = 2 * count * group + row
            values = [
                jnp.broadcast_to(table[:, n : n + 1], (half, lanes))
                for n in (first, first + count)
                for table in (cosines, sines)
            ]
            low = jnp.where(quarters == 0, values[0], values[1])
            high = jnp.where(quarters == 2, values[2], values[3])
            out_ref[group, row] = jnp.where(quarters < 2, low, high)


def close_kernel(mixed_ref, field_ref, out_ref, held_ref, sems):
    _, count, rows, _ = held_ref.shape
    depth = rows // STRIPS
    copies = []
    for strip in range(STRIPS):
        base = strip * depth
        own = pl.ds(base, depth)
        damping = jnp.exp(-0.5 * HALF_STEP * field_ref[own, :])
        low = low_lanes(damping.shape)
        for row in range(count):
            taken = pl.ds(base * count + row, depth, stride=count)
            first = mixed_ref[0, taken, :]
            second = mixed_ref[1, taken, :]
            held_ref[0, row, own, :] = jnp.where(low, first, swap(second)) * damping
            held_ref[1, row, own, :] = jnp.where(low, swap(first), second) * damping
        copy = pltpu.make_async_copy(held_ref.at[:, :, own], out_ref.at[:, :, own], sems.at[strip])
        copy.start()
        copies.append(copy)
    for copy in copies:
        copy.wait()


def whole(shape):
    return pl.BlockSpec(shape, lambda row: (0,) * len(shape))


def run_plane(propagator, plane, orientations, start):
    _, count, rows, cols = propagator.shape
    return pl.pallas_call(
        functools.partial(plane_kernel, count, start),
        grid=(count // BATCH,),
        in_specs=[
            pl.BlockSpec((2, BATCH, rows, cols), lambda row: (0, row, 0, 0)),
            whole((rows, cols)),
            whole(orientations.shape),
            whole((cols, cols)),
        ],
        out_specs=pl.BlockSpec((2, rows, BATCH, cols), lambda row: (0, 0, row, 0)),
        out_shape=jax.ShapeDtypeStruct((2, rows, count, cols), jnp.float32),
        scratch_shapes=[
            pltpu.VMEM((rows, cols), jnp.float32),
            pltpu.VMEM((2 * orientations.shape[1], cols), jnp.float32),
        ],
        compiler_params=LARGE,
        name="plane",
    )(propagator, plane, orientations, packed_tables(cols)[1])


def run_phase(orientations, groups, count, half, lanes):
    shape = jax.ShapeDtypeStruct((groups, count, half, lanes), jnp.float32)
    return pl.pallas_call(
        phase_kernel, out_shape=shape, compiler_params=SMALL, name="phase"
    )(orientations)


def run_line(lines, phases, matrix, total_z):
    groups, height, cols = lines.shape
    forward, inverse = packed_tables(total_z)
    pitch = groups * (height // total_z) + 8
    return pl.pallas_call(
        functools.partial(line_kernel, total_z),
        out_shape=jax.ShapeDtypeStruct(lines.shape, jnp.float32),
        scratch_shapes=[pltpu.VMEM((total_z * pitch, cols), jnp.float32)],
        compiler_params=SMALL,
        name="line",
    )(lines, wide_table(forward.T), wide_table(inverse), phases, matrix)


def run_close(mixed, plane, count):
    shape = (2, count) + plane.shape
    return pl.pallas_call(
        close_kernel,
        in_specs=[pl.BlockSpec(memory_space=pltpu.VMEM)] * 2,
        out_specs=pl.BlockSpec(memory_space=pl.ANY),
        out_shape=jax.ShapeDtypeStruct(shape, jnp.float32),
        scratch_shapes=[pltpu.VMEM(shape, jnp.float32), pltpu.SemaphoreType.DMA((STRIPS,))],
        compiler_params=SMALL,
        name="close",
    )(mixed, plane)


def local(propagator, field, orientations, weights):
    own, depth, rows, cols = propagator.shape
    groups = lax.axis_size("orient")
    slabs = lax.axis_size("slab")
    total_z = depth * slabs
    count = own // 2
    plane = field[0]
    sent = run_plane(
        propagator.reshape(2, count, rows, cols), plane, orientations, lambda: lax.axis_index("orient") * own
    )
    lines = lax.all_to_all(sent.reshape(groups * slabs, count, cols), AXES, 0, 0, tiled=True)
    phases = run_phase(orientations, groups, count, total_z // 2, cols)
    matrix = mixing_matrix(orientations, weights)
    matrix = matrix.reshape(groups, 2, count, groups, 2, count).transpose(1, 0, 2, 4, 3, 5)
    matrix = matrix.reshape(2 * own, 2 * own)
    message = (groups, slabs * count, cols)
    back = run_line(lines.reshape(message), phases, matrix, total_z)
    mixed = lax.all_to_all(back.reshape(groups * slabs, count, cols), AXES, 0, 0, tiled=True)
    result = run_close(mixed.reshape(message), plane, count)
    return result.reshape(own, 1, rows, cols)


def solution(mesh):
    in_specs = (P("orient", "slab", None, None), P("slab", None, None), P(), P())
    out_specs = P("orient", "slab", None, None)
    return jax.shard_map(local, mesh=mesh, in_specs=in_specs, out_specs=out_specs, check_vma=False)
```

```python
import functools
import math

import jax
import jax.numpy as jnp
import numpy as np
from jax import lax
from jax.experimental import pallas as pl
from jax.experimental.pallas import tpu as pltpu
from jax.sharding import PartitionSpec as P

LMAX = 10


HALF_STEP = 0.1
BOX_LENGTH = 12.8
DECAY_RATE = 0.01
HIGHEST = lax.Precision.HIGHEST
AXES = ("orient", "slab")
SMALL = pltpu.CompilerParams(vmem_limit_bytes=16 * 1024 * 1024)
LARGE = pltpu.CompilerParams()
BATCH = 8
STRIPS = 8
MIX_UNROLL = 32


def packed_tables(length):
    half = length // 2
    positions = np.arange(length)
    orders = np.arange(half)
    angles = (positions[:, None] * orders[None, :] % length) * (2.0 * math.pi / length)
    nyquist = np.where(positions % 2 == 0, 1.0, -1.0)
    sines = np.where(orders[None, :] == 0, nyquist[:, None], np.sin(angles))
    forward = np.concatenate([np.cos(angles), sines], axis=1)
    scale = np.where(np.arange(length) % half == 0, 1.0, 2.0) / length
    return forward.astype(np.float32), (forward * scale[None, :]).astype(np.float32)


def mixing_matrix(orientations, weights):
    cosines = jnp.dot(orientations.T, orientations, precision=HIGHEST)
    previous = jnp.ones_like(cosines)
    current = cosines
    combined = previous * (1.0 / (4.0 * math.pi))
    for degree in range(1, LMAX + 1):
        if degree > 1:
            previous, current = (
                current,
                ((2 * degree - 1) * cosines * current - (degree - 1) * previous) / degree,
            )
        combined = (
            combined
            + math.exp(-DECAY_RATE * degree * (degree + 1))
            * (2 * degree + 1)
            / (4.0 * math.pi)
            * current
        )
    return combined * weights[None, :]


def halves(values):
    high = values.astype(jnp.bfloat16)
    return high, (values - high.astype(jnp.float32)).astype(jnp.bfloat16)


def wide_table(values):
    high = values.astype(jnp.bfloat16)
    low = (values - high.astype(np.float32)).astype(jnp.bfloat16)
    return np.concatenate([high, high, low], axis=1)


def wide_left(values):
    high, low = halves(values)
    return jnp.concatenate([high, high, low], axis=1)


def wide_right(values):
    high, low = halves(values)
    return jnp.concatenate([high, low, high], axis=0)


def product(left, right):
    return jnp.dot(left, right, preferred_element_type=jnp.float32)


def swap(values):
    return pltpu.roll(values, values.shape[1] // 2, 1)


def low_lanes(shape):
    return lax.broadcasted_iota(jnp.int32, shape, 1) < shape[1] // 2


def circulant(row):
    length = row.shape[1]
    return pltpu.roll(jnp.broadcast_to(row, (length, length)), 0, 1, stride=1, stride_axis=0)


def narrow_product(left, right):
    left_high, left_low = halves(left)
    high, low = halves(right)
    top = jnp.concatenate([high, low], axis=1)
    bottom = jnp.concatenate([high, jnp.zeros_like(low)], axis=1)
    both = product(
        jnp.concatenate([left_high, left_low], axis=1), jnp.concatenate([top, bottom], axis=0)
    )
    columns = right.shape[1]
    return both[:, :columns] + both[:, columns:]


def shift_rows(orientations, inverse):
    length = inverse.shape[0]
    half = length // 2
    components = jnp.concatenate([orientations[0:1], -orientations[1:2]], axis=1)
    orders = lax.broadcasted_iota(jnp.int32, (half, components.shape[1]), 0)
    angles = components * (orders.astype(jnp.float32) * (HALF_STEP * 2.0 * math.pi / BOX_LENGTH))
    sines = jnp.where(orders == 0, 1.0, jnp.sin(angles))
    waves = jnp.concatenate([jnp.cos(angles), sines], axis=0)
    return narrow_product(inverse, waves).T


def plane_kernel(count, start, propagator_ref, field_ref, orientations_ref, inverse_ref, out_ref, damping_ref, rows_ref):
    step = pl.program_id(0)
    batch = propagator_ref.shape[1]
    total = rows_ref.shape[0] // 2
    first_own = start()

    @pl.when(step == 0)
    def _():
        damping_ref[...] = jnp.exp(-0.5 * HALF_STEP * field_ref[...])
        rows_ref[...] = shift_rows(orientations_ref[...], inverse_ref[...])

    for n in range(batch):
        row = step * batch + n
        moved = []
        for part in range(2):
            own = first_own + part * count + row
            damped = propagator_ref[part, n] * damping_ref[...]
            shift_x = circulant(rows_ref[pl.ds(own, 1), :])
            shift_y = circulant(rows_ref[pl.ds(total + own, 1), :])
            moved.append(narrow_product(shift_y, narrow_product(damped, shift_x)))
        first, second = moved
        low = low_lanes(first.shape)
        second = swap(second)
        out_ref[0, :, n, :] = jnp.where(low, first, second)
        out_ref[1, :, n, :] = jnp.where(low, second, first)


def line_kernel(depth, lines_ref, forward_ref, inverse_ref, phases_ref, mixing_ref, out_ref, advected_ref):
    groups = lines_ref.shape[0]
    count = lines_ref.shape[1] // depth
    half = depth // 2
    lanes = lines_ref.shape[2]
    pitch = advected_ref.shape[0] // depth
    quarter = lanes // 4
    even = (lax.broadcasted_iota(jnp.int32, (half, lanes), 1) // quarter) % 2 == 0

    def spread(group, row):
        packed = phases_ref[group, row]
        return (
            jnp.where(even, packed, pltpu.roll(packed, quarter, 1)),
            jnp.where(even, pltpu.roll(packed, lanes - quarter, 1), packed),
        )

    for group in range(groups):
        for row in range(0, count, 2):
            taken = [lines_ref[group, pl.ds(row + n, depth, stride=count), :] for n in range(2)]
            spectrum = product(forward_ref[...], wide_right(jnp.concatenate(taken, axis=1)))
            cosines, sines = (
                jnp.concatenate(tables, axis=1) for tables in zip(*(spread(group, row + n) for n in range(2)))
            )
            real, imaginary = spectrum[:half], spectrum[half:]
            turned = jnp.concatenate(
                [real * cosines - imaginary * sines, real * sines + imaginary * cosines], axis=0
            )
            advected = product(inverse_ref[...], wide_right(turned))
            for n in range(2):
                rows = pl.ds(group * count + row + n, depth, stride=pitch)
                advected_ref[rows, :] = advected[:, n * lanes : (n + 1) * lanes]

    both = 2 * count
    mixing = wide_left(mixing_ref[...])
    low = low_lanes((both, lanes))

    def mix(step, carry):
        stacked = []
        for n in range(2):
            base = (4 * step + 2 * n) * pitch
            first = advected_ref[pl.ds(base, both), :]
            second = advected_ref[pl.ds(base + pitch, both), :]
            stacked.append(
                jnp.concatenate(
                    [jnp.where(low, first, swap(second)), jnp.where(low, swap(first), second)], axis=0
                )
            )
        mixed = product(mixing, wide_right(jnp.concatenate(stacked, axis=1)))
        for n in range(2):
            place = mixed[:, n * lanes : (n + 1) * lanes]
            first, second = place[:both], swap(place[both:])
            for m, values in enumerate((jnp.where(low, first, second), jnp.where(low, second, first))):
                target = pl.ds((4 * step + 2 * n + m) * count, count)
                out_ref[0, target, :] = values[:count]
                out_ref[1, target, :] = values[count:]
        return carry

    lax.fori_loop(0, depth // 4, mix, 0, unroll=MIX_UNROLL)


def phase_kernel(orientations_ref, out_ref):
    groups, count, half, lanes = out_ref.shape
    component = orientations_ref[2:3, :]
    orders = lax.broadcasted_iota(jnp.int32, (half, component.shape[1]), 0)
    angles = component * (orders.astype(jnp.float32) * (HALF_STEP * 2.0 * math.pi / BOX_LENGTH))
    cosines, sines = jnp.cos(angles), jnp.sin(angles)
    quarters = lax.broadcasted_iota(jnp.int32, (half, lanes), 1) // (lanes // 4)
    for group in range(groups):
        for row in range(count):
            first = count * group + row
            values = [
                jnp.broadcast_to(table[:, n : n + 1], (half, lanes))
                for n in (first, first + groups * count)
                for table in (cosines, sines)
            ]
            low = jnp.where(quarters == 0, values[0], values[1])
            high = jnp.where(quarters == 2, values[2], values[3])
            out_ref[group, row] = jnp.where(quarters < 2, low, high)


def close_kernel(turned, mixed_ref, field_ref, out_ref, held_ref, sems):
    _, count, rows, _ = held_ref.shape
    depth = rows // STRIPS
    part = turned()
    copies = []
    for strip in range(STRIPS):
        base = strip * depth
        own = pl.ds(base, depth)
        damping = jnp.exp(-0.5 * HALF_STEP * field_ref[own, :])
        low = low_lanes(damping.shape)
        for row in range(count):
            taken = pl.ds(base * count + row, depth, stride=count)
            first = mixed_ref[0, taken, :]
            second = mixed_ref[1, taken, :]
            held_ref[part, row, own, :] = jnp.where(low, first, second) * damping
            held_ref[1 - part, row, own, :] = swap(jnp.where(low, second, first)) * damping
        copy = pltpu.make_async_copy(held_ref.at[:, :, own], out_ref.at[:, :, own], sems.at[strip])
        copy.start()
        copies.append(copy)
    for copy in copies:
        copy.wait()


def whole(shape):
    return pl.BlockSpec(shape, lambda row: (0,) * len(shape))


def run_plane(propagator, plane, orientations, start):
    _, count, rows, cols = propagator.shape
    return pl.pallas_call(
        functools.partial(plane_kernel, count, start),
        grid=(count // BATCH,),
        in_specs=[
            pl.BlockSpec((2, BATCH, rows, cols), lambda row: (0, row, 0, 0)),
            whole((rows, cols)),
            whole(orientations.shape),
            whole((cols, cols)),
        ],
        out_specs=pl.BlockSpec((2, rows, BATCH, cols), lambda row: (0, 0, row, 0)),
        out_shape=jax.ShapeDtypeStruct((2, rows, count, cols), jnp.float32),
        scratch_shapes=[
            pltpu.VMEM((rows, cols), jnp.float32),
            pltpu.VMEM((2 * orientations.shape[1], cols), jnp.float32),
        ],
        compiler_params=LARGE,
        name="plane",
    )(propagator, plane, orientations, packed_tables(cols)[1])


def run_phase(orientations, groups, count, half, lanes):
    shape = jax.ShapeDtypeStruct((groups, count, half, lanes), jnp.float32)
    return pl.pallas_call(
        phase_kernel, out_shape=shape, compiler_params=SMALL, name="phase"
    )(orientations)


def run_line(lines, phases, matrix, total_z):
    groups, height, cols = lines.shape
    forward, inverse = packed_tables(total_z)
    pitch = groups * (height // total_z) + 8
    return pl.pallas_call(
        functools.partial(line_kernel, total_z),
        out_shape=jax.ShapeDtypeStruct(lines.shape, jnp.float32),
        scratch_shapes=[pltpu.VMEM((total_z * pitch, cols), jnp.float32)],
        compiler_params=SMALL,
        name="line",
    )(lines, wide_table(forward.T), wide_table(inverse), phases, matrix)


def run_close(mixed, plane, count, turned):
    shape = (2, count) + plane.shape
    return pl.pallas_call(
        functools.partial(close_kernel, turned),
        in_specs=[pl.BlockSpec(memory_space=pltpu.VMEM)] * 2,
        out_specs=pl.BlockSpec(memory_space=pl.ANY),
        out_shape=jax.ShapeDtypeStruct(shape, jnp.float32),
        scratch_shapes=[pltpu.VMEM(shape, jnp.float32), pltpu.SemaphoreType.DMA((STRIPS,))],
        compiler_params=SMALL,
        name="close",
    )(mixed, plane)


def local(propagator, field, orientations, weights):
    own, depth, rows, cols = propagator.shape
    groups = lax.axis_size("orient")
    slabs = lax.axis_size("slab")
    total_z = depth * slabs
    count = own // 2
    plane = field[0]
    sent = run_plane(
        propagator.reshape(2, count, rows, cols), plane, orientations, lambda: lax.axis_index("orient") * own
    )
    lines = lax.all_to_all(sent.reshape(groups * slabs, count, cols), AXES, 0, 0, tiled=True)
    second_group = lax.axis_index("orient") == 1

    def listed(values):
        values = jnp.swapaxes(values.reshape(-1, groups, 2, count), 1, 2)
        values = jnp.where(second_group, values[:, ::-1], values)
        return values.reshape(-1, groups * own)

    directions = listed(orientations)
    phases = run_phase(directions, groups, count, total_z // 2, cols)
    matrix = mixing_matrix(directions, listed(weights)[0])
    message = (groups, slabs * count, cols)
    back = run_line(lines.reshape(message), phases, matrix, total_z)
    mixed = lax.all_to_all(back.reshape(groups * slabs, count, cols), AXES, 0, 0, tiled=True)
    result = run_close(mixed.reshape(message), plane, count, lambda: lax.axis_index("slab") % 2)
    return result.reshape(own, 1, rows, cols)


def solution(mesh):
    in_specs = (P("orient", "slab", None, None), P("slab", None, None), P(), P())
    out_specs = P("orient", "slab", None, None)
    return jax.shard_map(local, mesh=mesh, in_specs=in_specs, out_specs=out_specs, check_vma=False)
```

```python
import functools
import math

import jax
import jax.numpy as jnp
import numpy as np
from jax import lax
from jax.experimental import pallas as pl
from jax.experimental.pallas import tpu as pltpu
from jax.sharding import PartitionSpec as P

LMAX = 10


HALF_STEP = 0.1
BOX_LENGTH = 12.8
DECAY_RATE = 0.01
HIGHEST = lax.Precision.HIGHEST
AXES = ("orient", "slab")
SMALL = pltpu.CompilerParams(vmem_limit_bytes=16 * 1024 * 1024)
LARGE = pltpu.CompilerParams()
BATCH = 8
STRIPS = 8
MIX_UNROLL = 32


def packed_tables(length):
    half = length // 2
    positions = np.arange(length)
    orders = np.arange(half)
    angles = (positions[:, None] * orders[None, :] % length) * (2.0 * math.pi / length)
    nyquist = np.where(positions % 2 == 0, 1.0, -1.0)
    sines = np.where(orders[None, :] == 0, nyquist[:, None], np.sin(angles))
    forward = np.concatenate([np.cos(angles), sines], axis=1)
    scale = np.where(np.arange(length) % half == 0, 1.0, 2.0) / length
    return forward.astype(np.float32), (forward * scale[None, :]).astype(np.float32)


def mixing_matrix(orientations, weights):
    cosines = jnp.dot(orientations.T, orientations, precision=HIGHEST)
    previous = jnp.ones_like(cosines)
    current = cosines
    combined = previous * (1.0 / (4.0 * math.pi))
    for degree in range(1, LMAX + 1):
        if degree > 1:
            previous, current = (
                current,
                ((2 * degree - 1) * cosines * current - (degree - 1) * previous) / degree,
            )
        combined = (
            combined
            + math.exp(-DECAY_RATE * degree * (degree + 1))
            * (2 * degree + 1)
            / (4.0 * math.pi)
            * current
        )
    return combined * weights[None, :]


def halves(values):
    high = values.astype(jnp.bfloat16)
    return high, (values - high.astype(jnp.float32)).astype(jnp.bfloat16)


def wide_table(values):
    high = values.astype(jnp.bfloat16)
    low = (values - high.astype(np.float32)).astype(jnp.bfloat16)
    return np.concatenate([high, high, low], axis=1)


def wide_left(values):
    high, low = halves(values)
    return jnp.concatenate([high, high, low], axis=1)


def wide_right(values):
    high, low = halves(values)
    return jnp.concatenate([high, low, high], axis=0)


def product(left, right):
    return jnp.dot(left, right, preferred_element_type=jnp.float32)


def swap(values):
    return pltpu.roll(values, values.shape[1] // 2, 1)


def low_lanes(shape):
    return lax.broadcasted_iota(jnp.int32, shape, 1) < shape[1] // 2


def circulant(row):
    length = row.shape[1]
    return pltpu.roll(jnp.broadcast_to(row, (length, length)), 0, 1, stride=1, stride_axis=0)


def narrow_product(left, right):
    left_high, left_low = halves(left)
    high, low = halves(right)
    top = jnp.concatenate([high, low], axis=1)
    bottom = jnp.concatenate([high, jnp.zeros_like(low)], axis=1)
    both = product(
        jnp.concatenate([left_high, left_low], axis=1), jnp.concatenate([top, bottom], axis=0)
    )
    columns = right.shape[1]
    return both[:, :columns] + both[:, columns:]


def shift_rows(orientations, inverse):
    length = inverse.shape[0]
    half = length // 2
    components = jnp.concatenate([orientations[0:1], -orientations[1:2]], axis=1)
    orders = lax.broadcasted_iota(jnp.int32, (half, components.shape[1]), 0)
    angles = components * (orders.astype(jnp.float32) * (HALF_STEP * 2.0 * math.pi / BOX_LENGTH))
    sines = jnp.where(orders == 0, 1.0, jnp.sin(angles))
    waves = jnp.concatenate([jnp.cos(angles), sines], axis=0)
    return narrow_product(inverse, waves).T


def plane_kernel(
    start, propagator_ref, field_ref, orientations_ref, inverse_ref, out_ref,
    held_ref, field_held, orientations_held, inverse_held, done_ref, rows_ref, sems, out_sems,
):
    _, count, rows, _ = held_ref.shape
    total = rows_ref.shape[0] // 2
    first_own = start()
    small = [
        pltpu.make_async_copy(source, target, sems.at[0, n])
        for n, (source, target) in enumerate(
            (
                (orientations_ref, orientations_held),
                (inverse_ref, inverse_held),
                (field_ref, field_held),
            )
        )
    ]
    pieces = [
        [
            pltpu.make_async_copy(
                propagator_ref.at[part, pl.ds(first, BATCH)],
                held_ref.at[part, pl.ds(first, BATCH)],
                sems.at[1 + first // BATCH, part],
            )
            for part in range(2)
        ]
        for first in range(0, count, BATCH)
    ]
    for copies in [small] + pieces:
        for copy in copies:
            copy.start()
    for copy in small:
        copy.wait()
    field_held[...] = jnp.exp(-0.5 * HALF_STEP * field_held[...])
    rows_ref[...] = shift_rows(orientations_held[...], inverse_held[...])
    leaving = []
    for piece, copies in enumerate(pieces):
        for copy in copies:
            copy.wait()
        for n in range(BATCH):
            row = piece * BATCH + n
            moved = []
            for part in range(2):
                own = first_own + part * count + row
                damped = held_ref[part, row] * field_held[...]
                shift_x = circulant(rows_ref[pl.ds(own, 1), :])
                shift_y = circulant(rows_ref[pl.ds(total + own, 1), :])
                moved.append(narrow_product(shift_y, narrow_product(damped, shift_x)))
            first, second = moved[0], swap(moved[1])
            low = low_lanes(first.shape)
            done_ref[0, :, row, :] = jnp.where(low, first, second)
            done_ref[1, :, row, :] = jnp.where(low, second, first)
        part = pl.ds(piece * BATCH, BATCH)
        leave = pltpu.make_async_copy(done_ref.at[:, :, part], out_ref.at[:, :, part], out_sems.at[piece])
        leave.start()
        leaving.append(leave)
    for leave in leaving:
        leave.wait()


def line_kernel(depth, lines_ref, forward_ref, inverse_ref, phases_ref, mixing_ref, out_ref, advected_ref):
    groups = lines_ref.shape[0]
    count = lines_ref.shape[1] // depth
    half = depth // 2
    lanes = lines_ref.shape[2]
    pitch = advected_ref.shape[0] // depth
    quarter = lanes // 4
    even = (lax.broadcasted_iota(jnp.int32, (half, lanes), 1) // quarter) % 2 == 0

    def spread(group, row):
        packed = phases_ref[group, row]
        return (
            jnp.where(even, packed, pltpu.roll(packed, quarter, 1)),
            jnp.where(even, pltpu.roll(packed, lanes - quarter, 1), packed),
        )

    for group in range(groups):
        for row in range(0, count, 2):
            taken = [lines_ref[group, pl.ds(row + n, depth, stride=count), :] for n in range(2)]
            spectrum = product(forward_ref[...], wide_right(jnp.concatenate(taken, axis=1)))
            cosines, sines = (
                jnp.concatenate(tables, axis=1) for tables in zip(*(spread(group, row + n) for n in range(2)))
            )
            real, imaginary = spectrum[:half], spectrum[half:]
            turned = jnp.concatenate(
                [real * cosines - imaginary * sines, real * sines + imaginary * cosines], axis=0
            )
            advected = product(inverse_ref[...], wide_right(turned))
            for n in range(2):
                rows = pl.ds(group * count + row + n, depth, stride=pitch)
                advected_ref[rows, :] = advected[:, n * lanes : (n + 1) * lanes]

    both = 2 * count
    mixing = wide_left(mixing_ref[...])
    low = low_lanes((both, lanes))

    def mix(step, carry):
        stacked = []
        for n in range(2):
            base = (4 * step + 2 * n) * pitch
            first = advected_ref[pl.ds(base, both), :]
            second = advected_ref[pl.ds(base + pitch, both), :]
            stacked.append(
                jnp.concatenate(
                    [jnp.where(low, first, swap(second)), jnp.where(low, swap(first), second)], axis=0
                )
            )
        mixed = product(mixing, wide_right(jnp.concatenate(stacked, axis=1)))
        for n in range(2):
            place = mixed[:, n * lanes : (n + 1) * lanes]
            first, second = place[:both], swap(place[both:])
            for m, values in enumerate((jnp.where(low, first, second), jnp.where(low, second, first))):
                target = pl.ds((4 * step + 2 * n + m) * count, count)
                out_ref[0, target, :] = values[:count]
                out_ref[1, target, :] = values[count:]
        return carry

    lax.fori_loop(0, depth // 4, mix, 0, unroll=MIX_UNROLL)


def phase_kernel(orientations_ref, out_ref):
    groups, count, half, lanes = out_ref.shape
    component = orientations_ref[2:3, :]
    orders = lax.broadcasted_iota(jnp.int32, (half, component.shape[1]), 0)
    angles = component * (orders.astype(jnp.float32) * (HALF_STEP * 2.0 * math.pi / BOX_LENGTH))
    cosines, sines = jnp.cos(angles), jnp.sin(angles)
    quarters = lax.broadcasted_iota(jnp.int32, (half, lanes), 1) // (lanes // 4)
    for group in range(groups):
        for row in range(count):
            first = count * group + row
            values = [
                jnp.broadcast_to(table[:, n : n + 1], (half, lanes))
                for n in (first, first + groups * count)
                for table in (cosines, sines)
            ]
            low = jnp.where(quarters == 0, values[0], values[1])
            high = jnp.where(quarters == 2, values[2], values[3])
            out_ref[group, row] = jnp.where(quarters < 2, low, high)


def close_kernel(turned, mixed_ref, field_ref, out_ref, held_ref, sems):
    _, count, rows, _ = held_ref.shape
    depth = rows // STRIPS
    part = turned()
    copies = []
    for strip in range(STRIPS):
        base = strip * depth
        own = pl.ds(base, depth)
        damping = jnp.exp(-0.5 * HALF_STEP * field_ref[own, :])
        low = low_lanes(damping.shape)
        for row in range(count):
            taken = pl.ds(base * count + row, depth, stride=count)
            first = mixed_ref[0, taken, :]
            second = mixed_ref[1, taken, :]
            held_ref[part, row, own, :] = jnp.where(low, first, second) * damping
            held_ref[1 - part, row, own, :] = swap(jnp.where(low, second, first)) * damping
        copy = pltpu.make_async_copy(held_ref.at[:, :, own], out_ref.at[:, :, own], sems.at[strip])
        copy.start()
        copies.append(copy)
    for copy in copies:
        copy.wait()


def whole(shape):
    return pl.BlockSpec(shape, lambda row: (0,) * len(shape))


def run_plane(propagator, plane, orientations, start):
    _, count, rows, cols = propagator.shape
    message = (2, rows, count, cols)
    return pl.pallas_call(
        functools.partial(plane_kernel, start),
        in_specs=[pl.BlockSpec(memory_space=pl.ANY)] * 4,
        out_specs=pl.BlockSpec(memory_space=pl.ANY),
        out_shape=jax.ShapeDtypeStruct(message, jnp.float32),
        scratch_shapes=[
            pltpu.VMEM(propagator.shape, jnp.float32),
            pltpu.VMEM((rows, cols), jnp.float32),
            pltpu.VMEM(orientations.shape, jnp.float32),
            pltpu.VMEM((cols, cols), jnp.float32),
            pltpu.VMEM(message, jnp.float32),
            pltpu.VMEM((2 * orientations.shape[1], cols), jnp.float32),
            pltpu.SemaphoreType.DMA((1 + count // BATCH, 3)),
            pltpu.SemaphoreType.DMA((count // BATCH,)),
        ],
        compiler_params=LARGE,
        name="plane",
    )(propagator, plane, orientations, packed_tables(cols)[1])


def run_phase(orientations, groups, count, half, lanes):
    shape = jax.ShapeDtypeStruct((groups, count, half, lanes), jnp.float32)
    return pl.pallas_call(
        phase_kernel, out_shape=shape, compiler_params=SMALL, name="phase"
    )(orientations)


def run_line(lines, phases, matrix, total_z):
    groups, height, cols = lines.shape
    forward, inverse = packed_tables(total_z)
    pitch = groups * (height // total_z) + 12
    return pl.pallas_call(
        functools.partial(line_kernel, total_z),
        out_shape=jax.ShapeDtypeStruct(lines.shape, jnp.float32),
        scratch_shapes=[pltpu.VMEM((total_z * pitch, cols), jnp.float32)],
        compiler_params=SMALL,
        name="line",
    )(lines, wide_table(forward.T), wide_table(inverse), phases, matrix)


def run_close(mixed, plane, count, turned):
    shape = (2, count) + plane.shape
    return pl.pallas_call(
        functools.partial(close_kernel, turned),
        in_specs=[pl.BlockSpec(memory_space=pltpu.VMEM)] * 2,
        out_specs=pl.BlockSpec(memory_space=pl.ANY),
        out_shape=jax.ShapeDtypeStruct(shape, jnp.float32),
        scratch_shapes=[pltpu.VMEM(shape, jnp.float32), pltpu.SemaphoreType.DMA((STRIPS,))],
        compiler_params=SMALL,
        name="close",
    )(mixed, plane)


def local(propagator, field, orientations, weights):
    own, depth, rows, cols = propagator.shape
    groups = lax.axis_size("orient")
    slabs = lax.axis_size("slab")
    total_z = depth * slabs
    count = own // 2
    plane = field[0]
    sent = run_plane(
        propagator.reshape(2, count, rows, cols), plane, orientations, lambda: lax.axis_index("orient") * own
    )
    lines = lax.all_to_all(sent.reshape(groups * slabs, count, cols), AXES, 0, 0, tiled=True)
    second_group = lax.axis_index("orient") == 1

    def listed(values):
        values = jnp.swapaxes(values.reshape(-1, groups, 2, count), 1, 2)
        values = jnp.where(second_group, values[:, ::-1], values)
        return values.reshape(-1, groups * own)

    directions = listed(orientations)
    phases = run_phase(directions, groups, count, total_z // 2, cols)
    matrix = mixing_matrix(directions, listed(weights)[0])
    message = (groups, slabs * count, cols)
    back = run_line(lines.reshape(message), phases, matrix, total_z)
    mixed = lax.all_to_all(back.reshape(groups * slabs, count, cols), AXES, 0, 0, tiled=True)
    result = run_close(mixed.reshape(message), plane, count, lambda: lax.axis_index("slab") % 2)
    return result.reshape(own, 1, rows, cols)


def solution(mesh):
    in_specs = (P("orient", "slab", None, None), P("slab", None, None), P(), P())
    out_specs = P("orient", "slab", None, None)
    return jax.shard_map(local, mesh=mesh, in_specs=in_specs, out_specs=out_specs, check_vma=False)
```

```python
import functools
import math

import jax
import jax.numpy as jnp
import numpy as np
from jax import lax
from jax.experimental import pallas as pl
from jax.experimental.pallas import tpu as pltpu
from jax.sharding import PartitionSpec as P

LMAX = 10


HALF_STEP = 0.1
BOX_LENGTH = 12.8
DECAY_RATE = 0.01
HIGHEST = lax.Precision.HIGHEST
AXES = ("orient", "slab")
SMALL = pltpu.CompilerParams(vmem_limit_bytes=16 * 1024 * 1024)
LARGE = pltpu.CompilerParams()
BATCH = 8
STRIPS = 8
MIX_UNROLL = 32


def packed_tables(length):
    half = length // 2
    positions = np.arange(length)
    orders = np.arange(half)
    angles = (positions[:, None] * orders[None, :] % length) * (2.0 * math.pi / length)
    nyquist = np.where(positions % 2 == 0, 1.0, -1.0)
    sines = np.where(orders[None, :] == 0, nyquist[:, None], np.sin(angles))
    forward = np.concatenate([np.cos(angles), sines], axis=1)
    scale = np.where(np.arange(length) % half == 0, 1.0, 2.0) / length
    return forward.astype(np.float32), (forward * scale[None, :]).astype(np.float32)


def mixing_matrix(orientations, weights):
    cosines = jnp.dot(orientations.T, orientations, precision=HIGHEST)
    previous = jnp.ones_like(cosines)
    current = cosines
    combined = previous * (1.0 / (4.0 * math.pi))
    for degree in range(1, LMAX + 1):
        if degree > 1:
            previous, current = (
                current,
                ((2 * degree - 1) * cosines * current - (degree - 1) * previous) / degree,
            )
        combined = (
            combined
            + math.exp(-DECAY_RATE * degree * (degree + 1))
            * (2 * degree + 1)
            / (4.0 * math.pi)
            * current
        )
    return combined * weights[None, :]


def halves(values):
    high = values.astype(jnp.bfloat16)
    return high, (values - high.astype(jnp.float32)).astype(jnp.bfloat16)


def wide_table(values):
    high = values.astype(jnp.bfloat16)
    low = (values - high.astype(np.float32)).astype(jnp.bfloat16)
    return np.concatenate([high, high, low], axis=1)


def wide_left(values):
    high, low = halves(values)
    return jnp.concatenate([high, high, low], axis=1)


def wide_right(values):
    high, low = halves(values)
    return jnp.concatenate([high, low, high], axis=0)


def product(left, right):
    return jnp.dot(left, right, preferred_element_type=jnp.float32)


def swap(values):
    return pltpu.roll(values, values.shape[1] // 2, 1)


def low_lanes(shape):
    return lax.broadcasted_iota(jnp.int32, shape, 1) < shape[1] // 2


def circulant(row):
    length = row.shape[1]
    return pltpu.roll(jnp.broadcast_to(row, (length, length)), 0, 1, stride=1, stride_axis=0)


def narrow_product(left, right):
    left_high, left_low = halves(left)
    high, low = halves(right)
    top = jnp.concatenate([high, low], axis=1)
    bottom = jnp.concatenate([high, jnp.zeros_like(low)], axis=1)
    both = product(
        jnp.concatenate([left_high, left_low], axis=1), jnp.concatenate([top, bottom], axis=0)
    )
    columns = right.shape[1]
    return both[:, :columns] + both[:, columns:]


def shift_rows(orientations, inverse):
    length = inverse.shape[0]
    half = length // 2
    components = jnp.concatenate([orientations[0:1], -orientations[1:2]], axis=1)
    orders = lax.broadcasted_iota(jnp.int32, (half, components.shape[1]), 0)
    angles = components * (orders.astype(jnp.float32) * (HALF_STEP * 2.0 * math.pi / BOX_LENGTH))
    sines = jnp.where(orders == 0, 1.0, jnp.sin(angles))
    waves = jnp.concatenate([jnp.cos(angles), sines], axis=0)
    return narrow_product(inverse, waves).T


def plane_kernel(count, start, propagator_ref, field_ref, orientations_ref, inverse_ref, out_ref, damping_ref, rows_ref):
    step = pl.program_id(0)
    batch = propagator_ref.shape[1]
    total = rows_ref.shape[0] // 2
    first_own = start()

    @pl.when(step == 0)
    def _():
        damping_ref[...] = jnp.exp(-0.5 * HALF_STEP * field_ref[...])
        rows_ref[...] = shift_rows(orientations_ref[...], inverse_ref[...])

    for n in range(batch):
        row = step * batch + n
        moved = []
        for part in range(2):
            own = first_own + part * count + row
            damped = propagator_ref[part, n] * damping_ref[...]
            shift_x = circulant(rows_ref[pl.ds(own, 1), :])
            shift_y = circulant(rows_ref[pl.ds(total + own, 1), :])
            moved.append(narrow_product(shift_y, narrow_product(damped, shift_x)))
        first, second = moved
        low = low_lanes(first.shape)
        second = swap(second)
        out_ref[0, :, n, :] = jnp.where(low, first, second)
        out_ref[1, :, n, :] = jnp.where(low, second, first)


def line_kernel(depth, lines_ref, forward_ref, inverse_ref, phases_ref, mixing_ref, out_ref, advected_ref):
    groups = lines_ref.shape[0]
    count = lines_ref.shape[1] // depth
    half = depth // 2
    lanes = lines_ref.shape[2]
    pitch = advected_ref.shape[0] // depth
    quarter = lanes // 4
    even = (lax.broadcasted_iota(jnp.int32, (half, lanes), 1) // quarter) % 2 == 0

    def spread(group, row):
        packed = phases_ref[group, row]
        return (
            jnp.where(even, packed, pltpu.roll(packed, quarter, 1)),
            jnp.where(even, pltpu.roll(packed, lanes - quarter, 1), packed),
        )

    for group in range(groups):
        for row in range(0, count, 2):
            taken = [lines_ref[group, pl.ds(row + n, depth, stride=count), :] for n in range(2)]
            spectrum = product(forward_ref[...], wide_right(jnp.concatenate(taken, axis=1)))
            cosines, sines = (
                jnp.concatenate(tables, axis=1) for tables in zip(*(spread(group, row + n) for n in range(2)))
            )
            real, imaginary = spectrum[:half], spectrum[half:]
            turned = jnp.concatenate(
                [real * cosines - imaginary * sines, real * sines + imaginary * cosines], axis=0
            )
            advected = product(inverse_ref[...], wide_right(turned))
            for n in range(2):
                rows = pl.ds(group * count + row + n, depth, stride=pitch)
                advected_ref[rows, :] = advected[:, n * lanes : (n + 1) * lanes]

    both = 2 * count
    mixing = wide_left(mixing_ref[...])
    low = low_lanes((both, lanes))

    def mix(step, carry):
        stacked = []
        for n in range(2):
            base = (4 * step + 2 * n) * pitch
            first = advected_ref[pl.ds(base, both), :]
            second = advected_ref[pl.ds(base + pitch, both), :]
            stacked.append(
                jnp.concatenate(
                    [jnp.where(low, first, swap(second)), jnp.where(low, swap(first), second)], axis=0
                )
            )
        mixed = product(mixing, wide_right(jnp.concatenate(stacked, axis=1)))
        for n in range(2):
            place = mixed[:, n * lanes : (n + 1) * lanes]
            first, second = place[:both], swap(place[both:])
            for m, values in enumerate((jnp.where(low, first, second), jnp.where(low, second, first))):
                target = pl.ds((4 * step + 2 * n + m) * count, count)
                out_ref[0, target, :] = values[:count]
                out_ref[1, target, :] = values[count:]
        return carry

    lax.fori_loop(0, depth // 4, mix, 0, unroll=MIX_UNROLL)


def phase_kernel(orientations_ref, out_ref):
    groups, count, half, lanes = out_ref.shape
    component = orientations_ref[2:3, :]
    orders = lax.broadcasted_iota(jnp.int32, (half, component.shape[1]), 0)
    angles = component * (orders.astype(jnp.float32) * (HALF_STEP * 2.0 * math.pi / BOX_LENGTH))
    cosines, sines = jnp.cos(angles), jnp.sin(angles)
    quarters = lax.broadcasted_iota(jnp.int32, (half, lanes), 1) // (lanes // 4)
    for group in range(groups):
        for row in range(count):
            first = count * group + row
            values = [
                jnp.broadcast_to(table[:, n : n + 1], (half, lanes))
                for n in (first, first + groups * count)
                for table in (cosines, sines)
            ]
            low = jnp.where(quarters == 0, values[0], values[1])
            high = jnp.where(quarters == 2, values[2], values[3])
            out_ref[group, row] = jnp.where(quarters < 2, low, high)


def close_kernel(turned, mixed_ref, field_ref, out_ref, held_ref, sems):
    _, count, rows, _ = held_ref.shape
    depth = rows // STRIPS
    part = turned()
    copies = []
    for strip in range(STRIPS):
        base = strip * depth
        own = pl.ds(base, depth)
        damping = jnp.exp(-0.5 * HALF_STEP * field_ref[own, :])
        low = low_lanes(damping.shape)
        for row in range(count):
            taken = pl.ds(base * count + row, depth, stride=count)
            first = mixed_ref[0, taken, :]
            second = mixed_ref[1, taken, :]
            held_ref[part, row, own, :] = jnp.where(low, first, second) * damping
            held_ref[1 - part, row, own, :] = swap(jnp.where(low, second, first)) * damping
        copy = pltpu.make_async_copy(held_ref.at[:, :, own], out_ref.at[:, :, own], sems.at[strip])
        copy.start()
        copies.append(copy)
    for copy in copies:
        copy.wait()


def whole(shape):
    return pl.BlockSpec(shape, lambda row: (0,) * len(shape))


def run_plane(propagator, plane, orientations, start):
    _, count, rows, cols = propagator.shape
    return pl.pallas_call(
        functools.partial(plane_kernel, count, start),
        grid=(count // BATCH,),
        in_specs=[
            pl.BlockSpec((2, BATCH, rows, cols), lambda row: (0, row, 0, 0)),
            whole((rows, cols)),
            whole(orientations.shape),
            whole((cols, cols)),
        ],
        out_specs=pl.BlockSpec((2, rows, BATCH, cols), lambda row: (0, 0, row, 0)),
        out_shape=jax.ShapeDtypeStruct((2, rows, count, cols), jnp.float32),
        scratch_shapes=[
            pltpu.VMEM((rows, cols), jnp.float32),
            pltpu.VMEM((2 * orientations.shape[1], cols), jnp.float32),
        ],
        compiler_params=LARGE,
        name="plane",
    )(propagator, plane, orientations, packed_tables(cols)[1])


def run_phase(orientations, groups, count, half, lanes):
    shape = jax.ShapeDtypeStruct((groups, count, half, lanes), jnp.float32)
    return pl.pallas_call(
        phase_kernel, out_shape=shape, compiler_params=SMALL, name="phase"
    )(orientations)


def run_line(lines, phases, matrix, total_z):
    groups, height, cols = lines.shape
    forward, inverse = packed_tables(total_z)
    pitch = groups * (height // total_z) + 12
    return pl.pallas_call(
        functools.partial(line_kernel, total_z),
        out_shape=jax.ShapeDtypeStruct(lines.shape, jnp.float32),
        scratch_shapes=[pltpu.VMEM((total_z * pitch, cols), jnp.float32)],
        compiler_params=SMALL,
        name="line",
    )(lines, wide_table(forward.T), wide_table(inverse), phases, matrix)


def run_close(mixed, plane, count, turned):
    shape = (2, count) + plane.shape
    return pl.pallas_call(
        functools.partial(close_kernel, turned),
        in_specs=[pl.BlockSpec(memory_space=pltpu.VMEM)] * 2,
        out_specs=pl.BlockSpec(memory_space=pl.ANY),
        out_shape=jax.ShapeDtypeStruct(shape, jnp.float32),
        scratch_shapes=[pltpu.VMEM(shape, jnp.float32), pltpu.SemaphoreType.DMA((STRIPS,))],
        compiler_params=SMALL,
        name="close",
    )(mixed, plane)


def local(propagator, field, orientations, weights):
    own, depth, rows, cols = propagator.shape
    groups = lax.axis_size("orient")
    slabs = lax.axis_size("slab")
    total_z = depth * slabs
    count = own // 2
    plane = field[0]
    sent = run_plane(
        propagator.reshape(2, count, rows, cols), plane, orientations, lambda: lax.axis_index("orient") * own
    )
    lines = lax.all_to_all(sent.reshape(groups * slabs, count, cols), AXES, 0, 0, tiled=True)
    second_group = lax.axis_index("orient") == 1

    def listed(values):
        values = jnp.swapaxes(values.reshape(-1, groups, 2, count), 1, 2)
        values = jnp.where(second_group, values[:, ::-1], values)
        return values.reshape(-1, groups * own)

    directions = listed(orientations)
    phases = run_phase(directions, groups, count, total_z // 2, cols)
    matrix = mixing_matrix(directions, listed(weights)[0])
    message = (groups, slabs * count, cols)
    back = run_line(lines.reshape(message), phases, matrix, total_z)
    mixed = lax.all_to_all(back.reshape(groups * slabs, count, cols), AXES, 0, 0, tiled=True)
    result = run_close(mixed.reshape(message), plane, count, lambda: lax.axis_index("slab") % 2)
    return result.reshape(own, 1, rows, cols)


def solution(mesh):
    in_specs = (P("orient", "slab", None, None), P("slab", None, None), P(), P())
    out_specs = P("orient", "slab", None, None)
    return jax.shard_map(local, mesh=mesh, in_specs=in_specs, out_specs=out_specs, check_vma=False)
```
